512 devices in a mesh: row: 16 (over z_lo, y), col: 32 (over z_hi, x, core).
Axes of the slice: x: 4, y: 4, z: 16 (z_hi: 4, z_lo: 4; z = z_hi * 4 + z_lo), core: 2. Of those that a mesh axis runs over, the one named last changes fastest.
Arguments:
- coupling: bfloat16 [512, 1024, 512], P(('row', 'col')), may hold values from -0.25 to 0.25
- kinv: bfloat16 [512, 512, 512], P(('row', 'col')), as said below
- counts: int32 [512], P(('row', 'col')), may hold values from 4 to 8, as said below
- granules: int32 [512, 8], P(('row', 'col')), may hold values from 0 to 127, as said below
- hessian: bfloat16 [16, 1024, 16384], P(None, 'col', 'row'), as said below
- reg: float32 [16384], P('row'), may hold values from 32 to 96
Outputs:
- trailing: float32 [16, 1024, 16384], P(None, 'col', 'row')
The draws below stay inside these ranges and needn't reach their ends.
Inputs may be any that keep to these rules, and one draw needn't show every extreme that they name: `counts`: each block couples to between half of 8 and 8 index blocks; some block couples to 8, some to 4. `granules`: row k lists 8 distinct index blocks, all in band k // 32, that is numbers band * 8 to band * 8 + 7. Each kinv[k] is symmetric positive definite. Reshaped to [16384, 16384], hessian is symmetric.
All inputs are finite; a program needn't handle non-finite values.
Results may differ from the reference program's by a relative error of at most 0.00035.
Values sent between devices are 32-bit elements; how exact they have to be, the bound alone decides.
A program may use at most 64 MiB of HBM per device.

```python
import math
import jax
import jax.numpy as jnp
from jax import lax

NG = 8
NB = 512
PW = 512
TR = 1024
NBAND = 16
NL = 16384
BLOCKS = 512


def draw_kinv(key, part):
    noise = jax.random.normal(jax.random.fold_in(key, 11), (BLOCKS, NB, NB), jnp.float32)
    symmetric = (noise + jnp.swapaxes(noise, 1, 2)) / (2.0 * jnp.sqrt(jnp.float32(NB)))
    matrix = 2.0 * jnp.eye(NB, dtype=jnp.float32)[None] + 0.7 * symmetric
    return matrix.astype(jnp.bfloat16)


def draw_counts(key, part):
    values = jax.random.randint(jax.random.fold_in(key, 21), (BLOCKS,), NG // 2, NG + 1)
    first = jax.random.randint(jax.random.fold_in(key, 22), (), 0, BLOCKS)
    second = (first + 1 + jax.random.randint(jax.random.fold_in(key, 23), (), 0, BLOCKS - 1)) % BLOCKS
    values = values.at[first].set(NG)
    values = values.at[second].set(NG // 2)
    return values.astype(jnp.int32)


def draw_granules(key, part):
    keys = jax.random.split(jax.random.fold_in(key, 31), BLOCKS)
    orders = jax.vmap(lambda one_key: jax.random.permutation(one_key, NG))(keys)
    band_ids = jnp.arange(BLOCKS, dtype=jnp.int32) // (BLOCKS // NBAND)
    return (orders.astype(jnp.int32) + band_ids[:, None] * NG).astype(jnp.int32)


def draw_hessian(key, part):
    factor_rank = PW // 2
    noise = jax.random.normal(jax.random.fold_in(key, 41), (NL, NL), jnp.float32)
    factor = jax.random.normal(jax.random.fold_in(key, 42), (NL, factor_rank), jnp.float32)
    gram = jnp.dot(factor, factor.T, precision=lax.Precision.HIGHEST, preferred_element_type=jnp.float32)
    matrix = 12.0 * (noise + noise.T) / jnp.sqrt(jnp.float32(2 * NL)) + 48.0 / factor_rank * gram
    return matrix.reshape(NBAND, TR, NL).astype(jnp.bfloat16)


def block_scale(stream_key, shape, cuts, least, largest):
    loudness = 1.0
    for axis_at, shards_of in cuts:
        steps = jax.random.uniform(jax.random.fold_in(jax.random.fold_in(stream_key, 6), axis_at), (shards_of,), jnp.float32, least / len(cuts), largest / len(cuts))
        loudness = loudness * jnp.repeat(jnp.exp(steps), shape[axis_at] // shards_of).reshape((-1,) + (1,) * (len(shape) - 1 - axis_at))
    return loudness


def bell_draw(stream_key, shape, deviation, bound, pieces=(), held_as=jnp.bfloat16):
    drawn = deviation * jax.random.normal(stream_key, shape, jnp.float32)
    if pieces:
        drawn = drawn * block_scale(stream_key, shape, pieces, -0.22, 0.18)
    return jnp.clip(drawn, -bound, bound).astype(held_as)


def setup_inputs(seed: int = 0) -> dict:
    splits = jax.random.split(jax.random.key(seed), 7)
    return {
        "coupling": bell_draw(splits[0], (BLOCKS, TR, NB), NB ** -0.5, 0.25, ((0, 512),)),
        "kinv": draw_kinv(jax.random.fold_in(splits[6], 71), 0),
        "counts": draw_counts(jax.random.fold_in(splits[6], 71), 0),
        "granules": draw_granules(jax.random.fold_in(splits[6], 71), 0),
        "hessian": draw_hessian(jax.random.fold_in(splits[6], 71), 0),
        "reg": jnp.clip(jnp.exp(math.log(96.0) - 1.0986123 * jax.random.uniform(splits[5], (NL,), jnp.float32) ** block_scale(splits[5], (NL,), ((0, 16),), -0.2, 0.2)), 32.0, 96.0),
    }


def block_contribution(coupling_rows, kinv_block, count_live, granule_local):
    band_width = coupling_rows.shape[0]
    order = coupling_rows.shape[1]
    granule_size = band_width // NG
    products = jnp.dot(coupling_rows.astype(jnp.float32), kinv_block.astype(jnp.float32), preferred_element_type=jnp.float32).astype(jnp.bfloat16)
    slots = jnp.arange(NG, dtype=jnp.int32)
    placed = (granule_local[None, :] == slots[:, None]) & (slots[None, :] < count_live)
    selector = placed.astype(jnp.float32)
    stacked = jnp.stack([coupling_rows, products]).reshape(2, NG, granule_size, order).astype(jnp.float32)
    embedded = jnp.einsum('ua,sagn->sugn', selector, stacked)
    embedded = embedded.astype(jnp.bfloat16).reshape(2, band_width, order)
    return lax.dot_general(embedded[0].astype(jnp.float32), embedded[1].astype(jnp.float32), (((1,), (1,)), ((), ())), preferred_element_type=jnp.float32)

def reference(coupling, kinv, counts, granules, hessian, reg):
    per_band = BLOCKS // NBAND

    def accumulate(index, bands):
        band_number = index // per_band
        local_ids = (granules[index] - band_number * NG).astype(jnp.int32)
        addition = block_contribution(coupling[index], kinv[index], counts[index], local_ids)
        return bands.at[band_number].add(addition)
    bands = lax.fori_loop(0, BLOCKS, accumulate, jnp.zeros((NBAND, TR, TR), jnp.float32))
    schur = hessian.astype(jnp.float32).reshape(NL, NL)
    for band_index in range(NBAND):
        first = band_index * TR
        schur = schur.at[first:first + TR, first:first + TR].add(bands[band_index])
    diagonal_ids = jnp.arange(NL, dtype=jnp.int32)
    schur = schur.at[diagonal_ids, diagonal_ids].add(reg)
    lower = jnp.linalg.cholesky(schur[:PW, :PW])
    upper = jax.scipy.linalg.solve_triangular(lower, schur[:PW, :], lower=True)
    update = lax.dot_general(upper.astype(jnp.float32), upper.astype(jnp.float32), (((0,), (0,)), ((), ())), precision=lax.Precision.HIGHEST, preferred_element_type=jnp.float32)
    keep = (diagonal_ids[:, None] >= PW) & (diagonal_ids[None, :] >= PW)
    return jnp.where(keep, schur - update, jnp.zeros((), jnp.float32)).reshape(NBAND, TR, NL)
```

```python
import jax
import jax.numpy as jnp
from jax import lax
from jax.experimental import pallas as pl
from jax.experimental.pallas import tpu as pltpu
from jax.sharding import PartitionSpec as P

PW = 512
MESH = pl.DeviceIdType.MESH
VM = pltpu.VMEM
F32 = jnp.float32
BF16 = jnp.bfloat16
HIGH = lax.Precision.HIGHEST


def in_hbm(a):
    return pltpu.with_memory_space_constraint(a, pltpu.HBM)


def embed_kernel(
    counts_ref, granules_ref, reg_hbm, coupling_hbm, kinv_hbm, emb_ref, diag_ref,
    coupling, kinv, reg, product, loads,
):
    row = lax.axis_index("row")
    col = lax.axis_index("col")
    fetches = [
        pltpu.make_async_copy(coupling_hbm, coupling, loads.at[0]),
        pltpu.make_async_copy(kinv_hbm, kinv, loads.at[1]),
        pltpu.make_async_copy(reg_hbm, reg, loads.at[2]),
    ]
    for fetch in fetches:
        fetch.start()
    for fetch in fetches:
        fetch.wait()
    diag_at = lax.broadcasted_iota(jnp.int32, (32, 1024), 0) + col * 32
    lane_at = lax.broadcasted_iota(jnp.int32, (32, 1024), 1)
    diag_ref[...] = jnp.where(diag_at == lane_at, reg[...], 0.0)
    product[...] = jnp.dot(coupling[...], kinv[...], preferred_element_type=F32).astype(BF16)
    m, n = 128, 512
    for u in range(8):
        slot, live = jnp.int32(0), jnp.int32(0)
        for slot_of in range(8):
            here = (granules_ref[0, slot_of] == row * 8 + u) & (slot_of < counts_ref[0])
            slot = jnp.where(here, slot_of, slot)
            live = jnp.where(here, 1, live)
        block = pl.ds(pl.multiple_of(slot * m, m), m)
        shown = jnp.full((m, n), live, jnp.int32) > 0
        for which, whole in enumerate((coupling, product)):
            emb_ref[which, u * m:(u + 1) * m, :] = jnp.where(shown, whole[block, :], jnp.zeros((m, n), BF16))


def embed(coupling, kinv, counts, granules, reg):
    smem, vmem, hbm = (pl.BlockSpec(memory_space=s) for s in (pltpu.SMEM, pltpu.VMEM, pltpu.HBM))
    return pl.pallas_call(
        embed_kernel,
        name="embed",
        out_shape=(
            jax.ShapeDtypeStruct((2, 1024, 512), BF16),
            jax.ShapeDtypeStruct((32, 1024), F32),
        ),
        in_specs=[smem, smem, hbm, hbm, hbm],
        out_specs=(vmem, vmem),
        scratch_shapes=[
            VM((1024, 512), BF16), VM((512, 512), BF16), VM((1, 1024), F32), VM((1024, 512), BF16),
            pltpu.SemaphoreType.DMA((3,)),
        ],
        compiler_params=pltpu.CompilerParams(vmem_limit_bytes=32 * 2**20),
    )(counts, granules, in_hbm(reg.reshape(1, 1024)), in_hbm(coupling), in_hbm(kinv))


def dot(a, b):
    return lax.dot_general(a, b, (((1,), (0,)), ((), ())), precision=HIGH, preferred_element_type=F32)


def factor_chunk(k, chunk_ref, out, held, done, gathered):
    m, w = 128, 32
    at = pl.multiple_of(k * m, m)
    tile_at = [pl.multiple_of(((k + o) % 4) * m, m) for o in range(4)]
    gathered[...] = dot(out[:, pl.ds(at, m)].T, out[...])
    out[:, pl.ds(at, m)] = jnp.zeros((out.shape[0], m), F32)
    for o in range(4):
        lanes = pl.ds(tile_at[o], m)
        given = chunk_ref[:, :, :, lanes].reshape(m, m)
        held[o] = jnp.where((k + o) % 4 >= k, given, 0.0) - gathered[:, lanes]
    lane = lax.broadcasted_iota(jnp.int32, (1, m), 1)
    for j in range(4):
        tiles = [[held[o, w * j + 8 * i:w * j + 8 * i + 8, :] for o in range(4)] for i in range(4)]
        for r in range(w):
            i0, sub, here = r // 8, r % 8, lane == w * j + r
            first = i0 + (sub == 7)
            factors = {
                i: jnp.broadcast_to(tiles[i][0][:, w * j + r:w * j + r + 1], (8, m)) for i in range(i0, 4)
            }
            pivot = factors[i0][sub:sub + 1, :]
            top = [t[sub:sub + 1, :] for t in tiles[i0]]
            top[0] = jnp.where(here, 1.0, top[0])
            inverse, root = 1.0 / pivot, jnp.sqrt(pivot)
            scaled = [t * inverse for t in top]
            for o in range(4):
                done[o, r:r + 1, :] = scaled[o] * root
            for i in range(first, 4):
                old = [jnp.where(here, 0.0, tiles[i][0])] + tiles[i][1:]
                tiles[i] = [old[o] - factors[i] * jnp.broadcast_to(scaled[o], (8, m)) for o in range(4)]
        for o in range(4):
            out[pl.ds(at + w * j, w), pl.ds(tile_at[o], m)] = done[o]
        if j < 3:
            turned = done[0].T
            gone = (lane >= w * j) & (lane < w * j + w)
            above = gone & (lane > w * j + lax.broadcasted_iota(jnp.int32, (w, 1), 0))
            wide = jnp.concatenate([jnp.where(above, 0.0, done[0])] + [done[o] for o in (1, 2, 3)], axis=1)
            cuts = (w * (j + 1), w * (j + 2), m) if j < 2 else (w * (j + 1), m)
            for lo, hi in zip(cuts, cuts[1:]):
                change = dot(turned[lo:hi], wide)
                for o in range(4):
                    old = held[o, lo:hi, :]
                    if o == 0:
                        old = jnp.where(gone, 0.0, old)
                    held[o, lo:hi, :] = old - change[:, m * o:m * (o + 1)]
    below = lane <= lax.broadcasted_iota(jnp.int32, (m, 1), 0)
    out[pl.ds(at, m), pl.ds(at, m)] = jnp.where(below, out[pl.ds(at, m), pl.ds(at, m)], 0.0)


CHUNKS = range(4)
ORDER = (2, 1, 3, 0)


def schur_kernel(
    emb_ref, diag_ref, hess_hbm,
    inv_ref, panel_ref, rows_ref, share_ref,
    hess_ref, load,
    part, dp, dr, core_in, core_sum, x_in, x_sum, z_in, piv,
    pc_in, pc_sum, px_in, pz, rc_in, rc_sum, rx_in, rz, ry, spare, held, done, gathered,
    s_core, r_core, s_x, r_x, s_z, r_z,
    s_fz, r_fz, s_fx, r_fx, s_fc, r_fc, s_gs, r_gs, s_gt, r_gt, s_gz, r_gz, s_gy, r_gy,
    s_pc, r_pc, s_px, r_px, s_pz, r_pz, s_rc, r_rc, s_rx, r_rx, s_rz, r_rz, s_ry, r_ry,
    s_vy, r_vy, s_vz, r_vz, s_vx, r_vx, s_vc, r_vc,
):
    row = lax.axis_index("row")
    col = lax.axis_index("col")
    zlo, y = row // 4, row % 4
    z, x, core = col // 8, (col // 2) % 4, col % 2
    other = 1 - core
    n, m = PW, 128
    first = row == 0

    def col_of(zz, xx, cc):
        return zz * 8 + xx * 2 + cc

    def row_of(ll, yy):
        return ll * 4 + yy

    def copy(src, dst, ss, rs, r, c):
        return pltpu.make_async_remote_copy(
            src_ref=src, dst_ref=dst, send_sem=ss, recv_sem=rs,
            device_id=(r, c), device_id_type=MESH,
        )

    def by_x(o):
        return row, col_of(z, (x + o) % 4, core)

    def by_z(e):
        return row, col_of((z + e) % 4, x, core)

    def by_y(o):
        return row_of(zlo, (y + o) % 4), col

    def by_l(o):
        return row_of((zlo + o) % 4, y), col

    pair = (row, col_of(z, x, other))

    def t_core(q):
        return copy(part.at[q, :, other], core_in.at[q], s_core.at[q], r_core.at[q], *pair)

    def t_x(q, o):
        return copy(core_sum.at[q, (x + o) % 4], x_in.at[o - 1, q], s_x.at[q, o - 1], r_x.at[q, o - 1], *by_x(o))

    def t_z(e):
        return copy(x_sum.at[(z + e) % 4], z_in.at[e - 1], s_z.at[e - 1], r_z.at[e - 1], *by_z(e))

    def t_fz(e):
        at = panel_ref.at[z % 2, x, core]
        return copy(at, at, s_fz.at[e - 1], r_fz.at[z % 2], *by_z(e))

    def got_fz(s):
        at = panel_ref.at[s, x, core]
        return copy(at, at, s_fz.at[0], r_fz.at[s], *by_z(1))

    def t_fx(s, o, xx):
        at = panel_ref.at[s, xx, core]
        return copy(at, at, s_fx.at[s, o - 1], r_fx.at[s, o - 1], *by_x(o))

    def t_fc(s, cc):
        at = panel_ref.at[s, :, cc]
        return copy(at, at, s_fc.at[s], r_fc.at[s], *pair)

    def t_gs(o, yy):
        return copy(spare.at[:, yy], rows_ref.at[:, yy], s_gs.at[o - 1], r_gs.at[0], *by_y(o))

    def t_gt(o, ll):
        at = rows_ref.at[ll, y]
        return copy(at, at, s_gt.at[o - 1], r_gt.at[0], *by_l(o))

    def t_gz(o, ll):
        at = rows_ref.at[ll, y]
        return copy(at, at, s_gz.at[o - 1], r_gz.at[o - 1], *by_l(o))

    def t_gy(l, o, yy):
        at = rows_ref.at[l, yy]
        return copy(at, at, s_gy.at[l, o - 1], r_gy.at[l, o - 1], *by_y(o))

    def t_pc(i):
        return copy(dp.at[i, :, other, :, m * i:n], pc_in.at[i, :, :, m * i:n], s_pc.at[i], r_pc.at[i], *pair)

    def t_px(i, o):
        return copy(pc_sum.at[i, (x + o) % 4, :, m * i:n], px_in.at[o - 1, i, :, m * i:n],
                    s_px.at[i, o - 1], r_px.at[i, o - 1], *by_x(o))

    def t_pz(i, e, zz):
        at = pz.at[zz, i, :, m * i:n]
        return copy(at, at, s_pz.at[i, e - 1], r_pz.at[i, e - 1], *by_z(e))

    def t_vy(i, o):
        at = piv.at[i, x, core, :, m * i:n]
        return copy(at, at, s_vy.at[i, o - 1], r_vy.at[i], *by_y(o))

    def t_vz(i, o):
        at = piv.at[i, x, core, :, m * i:n]
        return copy(at, at, s_vz.at[i, o - 1], r_vz.at[i], *by_l(o))

    def t_vx(i, o, xx):
        at = piv.at[i, xx, core, :, m * i:n]
        return copy(at, at, s_vx.at[i, o - 1], r_vx.at[i, o - 1], *by_x(o))

    def t_vc(i, cc):
        at = piv.at[i, :, cc, :, m * i:n]
        return copy(at, at, s_vc.at[i], r_vc.at[i], *pair)

    def t_rc(s):
        return copy(dr.at[s, :, other], rc_in.at[s], s_rc.at[s], r_rc.at[s], *pair)

    def t_rx(s, o):
        return copy(rc_sum.at[s, (x + o) % 4], rx_in.at[o - 1, s], s_rx.at[s, o - 1], r_rx.at[s, o - 1], *by_x(o))

    def t_rz(s, e, zz):
        at = rz.at[zz, s]
        return copy(at, at, s_rz.at[s, e - 1], r_rz.at[s, e - 1], *by_z(e))

    def t_ry(e):
        return copy(rz.at[z, (z + e) % 4], ry.at[e - 1], s_ry.at[e - 1], r_ry.at[e - 1], *by_z(e))

    def outer(p, q):
        return lax.dot_general(p, q, (((1,), (1,)), ((), ())), preferred_element_type=F32)

    fetch = pltpu.make_async_copy(hess_hbm, hess_ref, load)
    fetch.start()
    barrier = pltpu.get_barrier_semaphore()

    def greet(device):
        pl.semaphore_signal(barrier, inc=1, device_id=device, device_id_type=MESH)

    greet(pair)
    for o in (1, 2, 3):
        greet(by_z(o))
        greet(by_x(o))
        greet(by_y(o))
        greet(by_l(o))

    fetch.wait()

    @pl.when(first)
    def _():
        both = outer(emb_ref[0, 0:n], emb_ref[1, 0:n]) + outer(emb_ref[1, 0:n], emb_ref[0, 0:n])
        row_block = lax.broadcasted_iota(jnp.int32, (16, 1, 1), 0)
        held_here = (hess_ref[0, :, 0:n].astype(F32) + diag_ref[:, 0:n])[None]
        both = 0.5 * both.reshape(16, 32, n) + jnp.where(row_block == col, held_here, 0.0)
        dp[...] = both.reshape(4, 4, 2, 16, n)
        dr[0:2] = outer(emb_ref[0, 0:n], emb_ref[1, n:2 * n]).reshape(2, 4, 2, 32, n)
        dr[2:4] = outer(emb_ref[1, n:2 * n], emb_ref[0, 0:n]).reshape(2, 4, 2, 32, n)
        for l in range(4):
            for yy in range(4):
                to = spare if yy else rows_ref
                to[l, yy] = hess_ref[4 * l + yy, :, 0:n].astype(F32)
        for s in (0, 1):
            panel_ref[s, x, core, :, 0:n] = jnp.zeros((32, n), F32)

    @pl.when((row != 0) & (z < 2))
    def _():
        panel_ref[z % 2, x, core] = hess_ref[0].astype(F32)

    def contribute(q, _):
        rows_at = pl.ds(pl.multiple_of(q * 256, 256), 256)
        part[q] = outer(emb_ref[0, rows_at], emb_ref[1]).reshape(4, 2, 32, 2 * n)
        return 0

    lax.fori_loop(0, 4, contribute, 0)
    inv_ref[...] = jnp.zeros((n, n), F32)
    pl.semaphore_wait(barrier, 13)

    @pl.when(first)
    def _():
        for i in CHUNKS:
            t_pc(i).start()
        for s in range(4):
            t_rc(s).start()
        for o in (2, 1, 3):
            t_gs(o, (y + o) % 4).start()

    @pl.when((row != 0) & (z < 2))
    def _():
        for e in (2, 1, 3):
            t_fz(e).start()

    for q in range(4):
        t_core(q).start()

    @pl.when(first)
    def _():
        for o in (3, 2, 1):
            t_gt(o, (zlo + o) % 4).start()
        for i in CHUNKS:
            t_pc(i).wait_recv()
            lanes = slice(m * i, n)
            pc_sum[i, :, :, lanes] = dp[i, :, core, :, lanes] + pc_in[i, :, :, lanes]
            for o in (2, 1, 3):
                t_px(i, o).start()
        for s in range(4):
            t_rc(s).wait_recv()
            rc_sum[s] = dr[s, :, core] + rc_in[s]
            for o in (2, 1, 3):
                t_rx(s, o).start()
        for i in CHUNKS:
            for o in (1, 2, 3):
                t_px(i, o).wait_recv()
            lanes = slice(m * i, n)
            pz[z, i, :, lanes] = (pc_sum[i, x, :, lanes] + px_in[0, i, :, lanes]) + (
                px_in[1, i, :, lanes] + px_in[2, i, :, lanes])
            for e in (2, 1, 3):
                t_pz(i, e, z).start()
        for s in range(4):
            for o in (1, 2, 3):
                t_rx(s, o).wait_recv()
            summed = (rc_sum[s, x] + rx_in[0, s]) + (rx_in[1, s] + rx_in[2, s])
            if s < 2:
                summed = summed + jnp.where(z == s, hess_ref[0, :, n:2 * n].astype(F32), 0.0)
            rz[z, s] = summed
            if s < 2:
                for e in (2, 1, 3):
                    t_rz(s, e, z).start()
        for e in (2, 1, 3):
            @pl.when((z + e) % 4 >= 2)
            def _(e=e):
                t_ry(e).start()

    def combine(q, _):
        t_core(q).wait_recv()
        core_sum[q] = part[q, :, core] + core_in[q]
        for o in (2, 1, 3):
            t_x(q, o).start()
        return 0

    lax.fori_loop(0, 4, combine, 0)

    @pl.when(first)
    def _():
        for i in CHUNKS:
            for e in (1, 2, 3):
                t_pz(i, e, (z - e) % 4).wait_recv()
            lanes = slice(m * i, n)
            piv[i, x, core, :, lanes] = (pz[0, i, :, lanes] + pz[1, i, :, lanes]) + (
                pz[2, i, :, lanes] + pz[3, i, :, lanes])
            for o in (2, 1, 3):
                t_vy(i, o).start()
            for o in (3, 2, 1):
                t_vz(i, o).start()

    @pl.when((zlo == 0) & (y != 0))
    def _():
        t_gs(1, y).wait_recv()
        for o in (3, 2, 1):
            t_gt(o, (zlo + o) % 4).start()
            t_gz(o, zlo).start()

    for i in CHUNKS:
        @pl.when((zlo == 0) & (y != 0))
        def _(i=i):
            t_vy(i, 1).wait_recv()
            for o in (3, 2, 1):
                t_vz(i, o).start()

        @pl.when(zlo != 0)
        def _(i=i):
            t_vz(i, 1).wait_recv()

        for o in (2, 1, 3):
            t_vx(i, o, x).start()

    @pl.when(first)
    def _():
        for s in (0, 1):
            for e in (1, 2, 3):
                t_rz(s, e, (z - e) % 4).wait_recv()
            panel_ref[s, x, core, :, n:2 * n] = (rz[0, s] + rz[1, s]) + (rz[2, s] + rz[3, s])

        @pl.when(z >= 2)
        def _():
            for e in (1, 2, 3):
                t_ry(e).wait_recv()
            rows_ref[0, 0] = rows_ref[0, 0] + ((rz[z, z] + ry[0]) + (ry[1] + ry[2]))

        for o in (3, 2, 1):
            t_gz(o, zlo).start()

    @pl.when(zlo != 0)
    def _():
        t_gt(1, zlo).wait_recv()
        for o in (1, 2, 3):
            @pl.when((zlo + o) % 4 != 0)
            def _(o=o):
                t_gz(o, zlo).start()

    for s in (0, 1):
        @pl.when((row != 0) & (z != s))
        def _(s=s):
            got_fz(s).wait_recv()
        for o in (2, 1, 3):
            t_fx(s, o, x).start()
    for i in CHUNKS:
        for o in (1, 2, 3):
            t_vx(i, o, (x - o) % 4).wait_recv()
        t_vc(i, core).start()

    def band_z():
        for e in ORDER:
            q = (z + e) % 4
            for o in (1, 2, 3):
                t_x(q, o).wait_recv()
            x_sum[q] = (core_sum[q, x] + x_in[0, q]) + (x_in[1, q] + x_in[2, q])
            if e:
                t_z(e).start()

    def spread():
        for o in (0, 1, 2, 3):
            l = (zlo - o) % 4
            if o:
                @pl.when(zlo != 0)
                def _(o=o, l=l):
                    t_gz(o, l).wait_recv()
            for v in (2, 1, 3):
                t_gy(l, v, y).start()

    def panel_core():
        for s in (0, 1):
            for o in (1, 2, 3):
                t_fx(s, o, (x - o) % 4).wait_recv()
            t_fc(s, core).start()

    def step(k, _):
        for i in CHUNKS:
            @pl.when(k == i)
            def _(i=i):
                t_vc(i, other).wait_recv()
        factor_chunk(k, piv.at[k], inv_ref, held, done, gathered)
        for kk, work in enumerate((band_z, spread, panel_core)):
            @pl.when(k == kk)
            def _(work=work):
                work()
        return 0

    lax.fori_loop(0, 4, step, 0)
    for e in (1, 2, 3):
        t_z(e).wait_recv()
    share_ref[...] = (x_sum[z] + z_in[0]) + (z_in[1] + z_in[2]) + diag_ref[...]
    for l in range(4):
        for o in (1, 2, 3):
            t_gy(l, o, (y - o) % 4).wait_recv()
    for s in (0, 1):
        t_fc(s, other).wait_recv()

    for e in ORDER:
        t_core(e).wait_send()
        for o in (1, 2, 3):
            t_x(e, o).wait_send()
        if e:
            t_z(e).wait_send()
    for s in (0, 1):
        for o in (1, 2, 3):
            t_fx(s, o, x).wait_send()
        t_fc(s, core).wait_send()
    for o in (1, 2, 3):
        for l in range(4):
            t_gy(l, o, y).wait_send()

        @pl.when((zlo == 0) | ((zlo + o) % 4 != 0))
        def _(o=o):
            t_gz(o, zlo).wait_send()
    for i in CHUNKS:
        for o in (1, 2, 3):
            t_vx(i, o, x).wait_send()
        t_vc(i, core).wait_send()

    @pl.when(zlo == 0)
    def _():
        for o in (1, 2, 3):
            t_gt(o, (zlo + o) % 4).wait_send()
            for i in CHUNKS:
                t_vz(i, o).wait_send()

    @pl.when((row != 0) & (z < 2))
    def _():
        for e in (1, 2, 3):
            t_fz(e).wait_send()

    @pl.when(first)
    def _():
        for o in (1, 2, 3):
            t_gs(o, (y + o) % 4).wait_send()
            for i in CHUNKS:
                t_px(i, o).wait_send()
                t_pz(i, o, z).wait_send()
                t_vy(i, o).wait_send()
            for s in range(4):
                t_rx(s, o).wait_send()
                if s < 2:
                    t_rz(s, o, z).wait_send()

            @pl.when((z + o) % 4 >= 2)
            def _(o=o):
                t_ry(o).wait_send()
        for i in CHUNKS:
            t_pc(i).wait_send()
        for s in range(4):
            t_rc(s).wait_send()


def schur(embedded, diag, hessian):
    spec = pl.BlockSpec(memory_space=pltpu.VMEM)
    dma = pltpu.SemaphoreType.DMA
    pair = lambda *s: [dma(s), dma(s)]
    return pl.pallas_call(
        schur_kernel,
        name="schur",
        out_shape=(
            jax.ShapeDtypeStruct((512, 512), F32),
            jax.ShapeDtypeStruct((2, 4, 2, 32, 1024), F32),
            jax.ShapeDtypeStruct((4, 4, 32, 512), F32),
            jax.ShapeDtypeStruct((32, 1024), F32),
        ),
        in_specs=[spec, spec, pl.BlockSpec(memory_space=pltpu.HBM)],
        out_specs=(spec,) * 4,
        scratch_shapes=[
            VM((16, 32, 1024), BF16), dma(()),
            VM((4, 4, 2, 32, 1024), F32), VM((4, 4, 2, 16, 512), F32), VM((4, 4, 2, 32, 512), F32),
            VM((4, 4, 32, 1024), F32), VM((4, 4, 32, 1024), F32),
            VM((3, 4, 32, 1024), F32), VM((4, 32, 1024), F32), VM((3, 32, 1024), F32),
            VM((4, 4, 2, 16, 512), F32),
            VM((4, 4, 16, 512), F32), VM((4, 4, 16, 512), F32), VM((3, 4, 16, 512), F32), VM((4, 4, 16, 512), F32),
            VM((4, 4, 32, 512), F32), VM((4, 4, 32, 512), F32), VM((3, 4, 32, 512), F32), VM((4, 4, 32, 512), F32),
            VM((3, 32, 512), F32), VM((4, 4, 32, 512), F32),
            VM((4, 128, 128), F32), VM((4, 32, 128), F32), VM((128, 512), F32),
            *pair(4), *pair(4, 3), *pair(3),
            dma((3,)), dma((2,)), *pair(2, 3), *pair(2),
            dma((3,)), dma((1,)), dma((3,)), dma((1,)), *pair(3), *pair(4, 3),
            *pair(4), *pair(4, 3), *pair(4, 3), *pair(4), *pair(4, 3), *pair(2, 3), *pair(3),
            dma((4, 3)), dma((4,)), dma((4, 3)), dma((4,)), *pair(4, 3), *pair(4),
        ],
        compiler_params=pltpu.CompilerParams(
            collective_id=0, has_side_effects=True, vmem_limit_bytes=40 * 2**20
        ),
    )(embedded, diag, in_hbm(hessian))


def split(a):
    hi = a.astype(BF16)
    return hi, (a - hi.astype(F32)).astype(BF16)


def dot3(a, b, trans=False):
    dims = (((1,), (1 if trans else 0,)), ((), ()))
    mm = lambda p, q: lax.dot_general(p, q, dims, preferred_element_type=F32)
    (ah, al), (bh, bl) = a, b
    return mm(ah, bh) + (mm(ah, bl) + mm(al, bh))


def apply_kernel(inv_ref, panel_ref, rows_ref, hess_ref, share_ref, out_ref, uh, ul, vh, vl):
    row = lax.axis_index("row")
    col = lax.axis_index("col")
    at = pl.program_id(0)

    @pl.when(at == 0)
    def _():
        inv = split(inv_ref[...])
        for j in range(4):
            h, l = split(dot3(inv, split(panel_ref[:, 256 * j:256 * (j + 1)])))
            uh[:, 256 * j:256 * (j + 1)] = h
            ul[:, 256 * j:256 * (j + 1)] = l
        for j in range(2):
            h, l = split(dot3(split(rows_ref[256 * j:256 * (j + 1), :]), inv, trans=True))
            vh[256 * j:256 * (j + 1), :] = h
            vl[256 * j:256 * (j + 1), :] = l

    rows = pl.ds(pl.multiple_of(at * 128, 128), 128)
    update = dot3((vh[rows, :], vl[rows, :]), (uh[...], ul[...]))
    lane = lax.broadcasted_iota(jnp.int32, (1, 1024), 1)
    for q in range(4):
        band = at * 4 + q
        schur = hess_ref[q].astype(F32) + jnp.where(band == row, share_ref[...], 0.0)
        keep = (band * 1024 + col * 32 >= PW) & (row * 1024 + lane >= PW)
        out_ref[q] = jnp.where(keep, schur - update[32 * q:32 * (q + 1), :], 0.0)


def apply(inv, panel, rows, hessian, share):
    whole = lambda *s: pl.BlockSpec(s, lambda i: (0,) * len(s))
    return pl.pallas_call(
        apply_kernel,
        name="apply",
        grid=(4,),
        out_shape=jax.ShapeDtypeStruct((16, 32, 1024), F32),
        in_specs=[
            whole(512, 512), whole(512, 1024), whole(512, 512),
            pl.BlockSpec((4, 32, 1024), lambda i: (i, 0, 0)), whole(32, 1024),
        ],
        out_specs=pl.BlockSpec((4, 32, 1024), lambda i: (i, 0, 0)),
        scratch_shapes=[VM((512, 1024), BF16), VM((512, 1024), BF16), VM((512, 512), BF16), VM((512, 512), BF16)],
        compiler_params=pltpu.CompilerParams(
            dimension_semantics=("arbitrary",), vmem_limit_bytes=40 * 2**20
        ),
    )(inv, panel, rows, hessian, share)


def local(coupling, kinv, counts, granules, hessian, reg):
    embedded, diag = embed(coupling[0], kinv[0], counts, granules, reg)
    inv, panel, rows, share = schur(embedded, diag, hessian)
    return apply(inv, panel.reshape(512, 1024), rows.reshape(512, 512), hessian, share)


def solution(mesh):
    return jax.shard_map(
        local,
        mesh=mesh,
        in_specs=(
            P(("row", "col"), None, None),
            P(("row", "col"), None, None),
            P(("row", "col")),
            P(("row", "col"), None),
            P(None, "col", "row"),
            P("row"),
        ),
        out_specs=P(None, "col", "row"),
        check_vma=False,
    )
```

```python
import jax
import jax.numpy as jnp
from jax import lax
from jax.experimental import pallas as pl
from jax.experimental.pallas import tpu as pltpu
from jax.sharding import PartitionSpec as P

PW = 512
MESH = pl.DeviceIdType.MESH
VM = pltpu.VMEM
F32 = jnp.float32
BF16 = jnp.bfloat16
HIGH = lax.Precision.HIGHEST


def in_hbm(a):
    return pltpu.with_memory_space_constraint(a, pltpu.HBM)


def embed_kernel(
    counts_ref, granules_ref, reg_hbm, coupling_hbm, kinv_hbm, emb_ref, diag_ref,
    coupling, kinv, reg, product, loads,
):
    row = lax.axis_index("row")
    col = lax.axis_index("col")
    fetches = [
        pltpu.make_async_copy(coupling_hbm, coupling, loads.at[0]),
        pltpu.make_async_copy(kinv_hbm, kinv, loads.at[1]),
        pltpu.make_async_copy(reg_hbm, reg, loads.at[2]),
    ]
    for fetch in fetches:
        fetch.start()
    for fetch in fetches:
        fetch.wait()
    diag_at = lax.broadcasted_iota(jnp.int32, (32, 1024), 0) + col * 32
    lane_at = lax.broadcasted_iota(jnp.int32, (32, 1024), 1)
    diag_ref[...] = jnp.where(diag_at == lane_at, reg[...], 0.0)
    product[...] = jnp.dot(coupling[...], kinv[...], preferred_element_type=F32).astype(BF16)
    m, n = 128, 512
    for u in range(8):
        slot, live = jnp.int32(0), jnp.int32(0)
        for slot_of in range(8):
            here = (granules_ref[0, slot_of] == row * 8 + u) & (slot_of < counts_ref[0])
            slot = jnp.where(here, slot_of, slot)
            live = jnp.where(here, 1, live)
        block = pl.ds(pl.multiple_of(slot * m, m), m)
        shown = jnp.full((m, n), live, jnp.int32) > 0
        for which, whole in enumerate((coupling, product)):
            emb_ref[which, u * m:(u + 1) * m, :] = jnp.where(shown, whole[block, :], jnp.zeros((m, n), BF16))


def embed(coupling, kinv, counts, granules, reg):
    smem, vmem, hbm = (pl.BlockSpec(memory_space=s) for s in (pltpu.SMEM, pltpu.VMEM, pltpu.HBM))
    return pl.pallas_call(
        embed_kernel,
        name="embed",
        out_shape=(
            jax.ShapeDtypeStruct((2, 1024, 512), BF16),
            jax.ShapeDtypeStruct((32, 1024), F32),
        ),
        in_specs=[smem, smem, hbm, hbm, hbm],
        out_specs=(vmem, vmem),
        scratch_shapes=[
            VM((1024, 512), BF16), VM((512, 512), BF16), VM((1, 1024), F32), VM((1024, 512), BF16),
            pltpu.SemaphoreType.DMA((3,)),
        ],
        compiler_params=pltpu.CompilerParams(vmem_limit_bytes=32 * 2**20),
    )(counts, granules, in_hbm(reg.reshape(1, 1024)), in_hbm(coupling), in_hbm(kinv))


def dot(a, b):
    return lax.dot_general(a, b, (((1,), (0,)), ((), ())), precision=HIGH, preferred_element_type=F32)


def factor_chunk(k, chunk_ref, out, held, done, gathered):
    m, w = 128, 32
    at = pl.multiple_of(k * m, m)
    tile_at = [pl.multiple_of(((k + o) % 4) * m, m) for o in range(4)]
    for before in range(4):
        @pl.when(k == before)
        def _(before=before):
            if before:
                gathered[...] = dot(out[0:m * before, m * before:m * (before + 1)].T, out[0:m * before, :])
            else:
                gathered[...] = jnp.zeros(gathered.shape, F32)
    out[:, pl.ds(at, m)] = jnp.zeros((out.shape[0], m), F32)
    for o in range(4):
        lanes = pl.ds(tile_at[o], m)
        given = chunk_ref[:, :, :, lanes].reshape(m, m)
        held[o] = jnp.where((k + o) % 4 >= k, given, 0.0) - gathered[:, lanes]
    lane = lax.broadcasted_iota(jnp.int32, (1, m), 1)
    for j in range(4):
        tiles = [[held[o, w * j + 8 * i:w * j + 8 * i + 8, :] for o in range(4)] for i in range(4)]
        for r in range(0, w, 2):
            i0, sub = r // 8, r % 8
            one, two = lane == w * j + r, lane == w * j + r + 1
            first = i0 + (sub == 6)
            f0, f1 = (
                {i: jnp.broadcast_to(tiles[i][0][:, w * j + c:w * j + c + 1], (8, m)) for i in range(i0, 4)}
                for c in (r, r + 1)
            )
            p, q, s = f0[i0][sub:sub + 1, :], f1[i0][sub:sub + 1, :], f1[i0][sub + 1:sub + 2, :]
            det = p * s - q * q
            inverse = jnp.broadcast_to(1.0 / det, (8, m))
            top = [t[sub:sub + 1, :] for t in tiles[i0]]
            low = [t[sub + 1:sub + 2, :] for t in tiles[i0]]
            top[0] = jnp.where(one, 1.0, jnp.where(two, 0.0, top[0]))
            low[0] = jnp.where(two, 1.0, jnp.where(one, 0.0, low[0]))
            u0 = [s * t - q * l for t, l in zip(top, low)]
            u1 = [p * l - q * t for t, l in zip(top, low)]
            root0, root1 = 1.0 / jnp.sqrt(p), 1.0 / jnp.sqrt(p * det)
            for o in range(4):
                done[o, r:r + 1, :] = top[o] * root0
                done[o, r + 1:r + 2, :] = u1[o] * root1
            b0 = [jnp.broadcast_to(u, (8, m)) for u in u0]
            b1 = [jnp.broadcast_to(u, (8, m)) for u in u1]
            for i in range(first, 4):
                old = [jnp.where(one | two, 0.0, tiles[i][0])] + tiles[i][1:]
                tiles[i] = [old[o] - inverse * (f0[i] * b0[o] + f1[i] * b1[o]) for o in range(4)]
        for o in range(4):
            out[pl.ds(at + w * j, w), pl.ds(tile_at[o], m)] = done[o]
        if j < 3:
            turned = done[0].T
            gone = (lane >= w * j) & (lane < w * j + w)
            above = gone & (lane > w * j + lax.broadcasted_iota(jnp.int32, (w, 1), 0))
            wide = jnp.concatenate([jnp.where(above, 0.0, done[0])] + [done[o] for o in (1, 2, 3)], axis=1)
            cuts = (w * (j + 1), w * (j + 2), m) if j < 2 else (w * (j + 1), m)
            for lo, hi in zip(cuts, cuts[1:]):
                change = dot(turned[lo:hi], wide)
                for o in range(4):
                    old = held[o, lo:hi, :]
                    if o == 0:
                        old = jnp.where(gone, 0.0, old)
                    held[o, lo:hi, :] = old - change[:, m * o:m * (o + 1)]
    below = lane <= lax.broadcasted_iota(jnp.int32, (m, 1), 0)
    out[pl.ds(at, m), pl.ds(at, m)] = jnp.where(below, out[pl.ds(at, m), pl.ds(at, m)], 0.0)


CHUNKS = range(4)
ORDER = (2, 1, 3, 0)


def schur_kernel(
    emb_ref, diag_ref, hess_hbm,
    inv_ref, panel_ref, rows_ref, share_ref,
    hess_ref, load,
    part, dp, dr, core_in, core_sum, x_in, x_sum, z_in, piv,
    pc_in, pc_sum, px_in, pz, rc_in, rc_sum, rx_in, rz, ry, spare, held, done, gathered,
    s_core, r_core, s_x, r_x, s_z, r_z,
    s_fz, r_fz, s_fx, r_fx, s_fc, r_fc, s_gs, r_gs, s_gt, r_gt, s_gz, r_gz, s_gy, r_gy,
    s_pc, r_pc, s_px, r_px, s_pz, r_pz, s_rc, r_rc, s_rx, r_rx, s_rz, r_rz, s_ry, r_ry,
    s_vy, r_vy, s_vz, r_vz, s_vx, r_vx, s_vc, r_vc,
):
    row = lax.axis_index("row")
    col = lax.axis_index("col")
    zlo, y = row // 4, row % 4
    z, x, core = col // 8, (col // 2) % 4, col % 2
    other = 1 - core
    n, m = PW, 128
    first = row == 0

    def col_of(zz, xx, cc):
        return zz * 8 + xx * 2 + cc

    def row_of(ll, yy):
        return ll * 4 + yy

    def copy(src, dst, ss, rs, r, c):
        return pltpu.make_async_remote_copy(
            src_ref=src, dst_ref=dst, send_sem=ss, recv_sem=rs,
            device_id=(r, c), device_id_type=MESH,
        )

    def by_x(o):
        return row, col_of(z, (x + o) % 4, core)

    def by_z(e):
        return row, col_of((z + e) % 4, x, core)

    def by_y(o):
        return row_of(zlo, (y + o) % 4), col

    def by_l(o):
        return row_of((zlo + o) % 4, y), col

    pair = (row, col_of(z, x, other))

    def t_core(q, lo=0):
        return copy(part.at[q, :, other, :, lo:2 * n], core_in.at[q, :, :, lo:2 * n], s_core.at[q], r_core.at[q], *pair)

    def t_x(q, o, lo=0):
        return copy(core_sum.at[q, (x + o) % 4, :, lo:2 * n], x_in.at[o - 1, q, :, lo:2 * n], s_x.at[q, o - 1], r_x.at[q, o - 1], *by_x(o))

    def t_z(e, lo=0):
        return copy(x_sum.at[(z + e) % 4, :, lo:2 * n], z_in.at[e - 1, :, lo:2 * n], s_z.at[e - 1], r_z.at[e - 1], *by_z(e))

    def t_fz(e):
        at = panel_ref.at[z % 2, x, core]
        return copy(at, at, s_fz.at[e - 1], r_fz.at[z % 2], *by_z(e))

    def got_fz(s):
        at = panel_ref.at[s, x, core]
        return copy(at, at, s_fz.at[0], r_fz.at[s], *by_z(1))

    def t_fx(s, o, xx, lo=0):
        at = panel_ref.at[s, xx, core, :, lo:2 * n]
        return copy(at, at, s_fx.at[s, o - 1], r_fx.at[s, o - 1], *by_x(o))

    def t_fc(s, cc, lo=0):
        at = panel_ref.at[s, :, cc, :, lo:2 * n]
        return copy(at, at, s_fc.at[s], r_fc.at[s], *pair)

    def t_gs(o, yy):
        return copy(spare.at[:, yy], rows_ref.at[:, yy], s_gs.at[o - 1], r_gs.at[0], *by_y(o))

    def t_gt(o, ll):
        at = rows_ref.at[ll, y]
        return copy(at, at, s_gt.at[o - 1], r_gt.at[0], *by_l(o))

    def t_gz(o, ll):
        at = rows_ref.at[ll, y]
        return copy(at, at, s_gz.at[o - 1], r_gz.at[o - 1], *by_l(o))

    def t_gy(l, o, yy):
        at = rows_ref.at[l, yy]
        return copy(at, at, s_gy.at[l, o - 1], r_gy.at[l, o - 1], *by_y(o))

    def t_pc(i):
        return copy(dp.at[i, :, other, :, m * i:n], pc_in.at[i, :, :, m * i:n], s_pc.at[i], r_pc.at[i], *pair)

    def t_px(i, o):
        return copy(pc_sum.at[i, (x + o) % 4, :, m * i:n], px_in.at[o - 1, i, :, m * i:n],
                    s_px.at[i, o - 1], r_px.at[i, o - 1], *by_x(o))

    def t_pz(i, e, zz):
        at = pz.at[zz, i, :, m * i:n]
        return copy(at, at, s_pz.at[i, e - 1], r_pz.at[i, e - 1], *by_z(e))

    def t_vy(i, o):
        at = piv.at[i, x, core, :, m * i:n]
        return copy(at, at, s_vy.at[i, o - 1], r_vy.at[i], *by_y(o))

    def t_vz(i, o):
        at = piv.at[i, x, core, :, m * i:n]
        return copy(at, at, s_vz.at[i, o - 1], r_vz.at[i], *by_l(o))

    def t_vx(i, o, xx):
        at = piv.at[i, xx, core, :, m * i:n]
        return copy(at, at, s_vx.at[i, o - 1], r_vx.at[i, o - 1], *by_x(o))

    def t_vc(i, cc):
        at = piv.at[i, :, cc, :, m * i:n]
        return copy(at, at, s_vc.at[i], r_vc.at[i], *pair)

    def t_rc(s):
        return copy(dr.at[s, :, other], rc_in.at[s], s_rc.at[s], r_rc.at[s], *pair)

    def t_rx(s, o):
        return copy(rc_sum.at[s, (x + o) % 4], rx_in.at[o - 1, s], s_rx.at[s, o - 1], r_rx.at[s, o - 1], *by_x(o))

    def t_rz(s, e, zz):
        at = rz.at[zz, s]
        return copy(at, at, s_rz.at[s, e - 1], r_rz.at[s, e - 1], *by_z(e))

    def t_ry(e):
        return copy(rz.at[z, (z + e) % 4], ry.at[e - 1], s_ry.at[e - 1], r_ry.at[e - 1], *by_z(e))

    def outer(p, q):
        return lax.dot_general(p, q, (((1,), (1,)), ((), ())), preferred_element_type=F32)

    fetch = pltpu.make_async_copy(hess_hbm, hess_ref, load)
    fetch.start()
    barrier = pltpu.get_barrier_semaphore()

    def greet(device):
        pl.semaphore_signal(barrier, inc=1, device_id=device, device_id_type=MESH)

    greet(pair)
    for o in (1, 2, 3):
        greet(by_z(o))
        greet(by_x(o))
        greet(by_y(o))
        greet(by_l(o))

    fetch.wait()

    @pl.when(first)
    def _():
        both = outer(emb_ref[0, 0:n], emb_ref[1, 0:n]) + outer(emb_ref[1, 0:n], emb_ref[0, 0:n])
        row_block = lax.broadcasted_iota(jnp.int32, (16, 1, 1), 0)
        held_here = (hess_ref[0, :, 0:n].astype(F32) + diag_ref[:, 0:n])[None]
        both = 0.5 * both.reshape(16, 32, n) + jnp.where(row_block == col, held_here, 0.0)
        dp[...] = both.reshape(4, 4, 2, 16, n)
        dr[0:2] = outer(emb_ref[0, 0:n], emb_ref[1, n:2 * n]).reshape(2, 4, 2, 32, n)
        dr[2:4] = outer(emb_ref[1, n:2 * n], emb_ref[0, 0:n]).reshape(2, 4, 2, 32, n)
        for l in range(4):
            for yy in range(4):
                to = spare if yy else rows_ref
                to[l, yy] = hess_ref[4 * l + yy, :, 0:n].astype(F32)
        panel_ref[:, :, :, :, 0:n] = jnp.zeros((2, 4, 2, 32, n), F32)

    @pl.when((row != 0) & (z < 2))
    def _():
        panel_ref[z % 2, x, core] = hess_ref[0].astype(F32)

    def contribute(q, _):
        rows_at = pl.ds(pl.multiple_of(q * 256, 256), 256)
        part[q] = outer(emb_ref[0, rows_at], emb_ref[1]).reshape(4, 2, 32, 2 * n)
        return 0

    lax.fori_loop(0, 4, contribute, 0)
    inv_ref[...] = jnp.zeros((n, n), F32)
    pl.semaphore_wait(barrier, 13)

    @pl.when(first)
    def _():
        for i in CHUNKS:
            t_pc(i).start()
        for s in range(4):
            t_rc(s).start()
        for o in (2, 1, 3):
            t_gs(o, (y + o) % 4).start()

    @pl.when((row != 0) & (z < 2))
    def _():
        for e in (2, 1, 3):
            t_fz(e).start()

    others = row != 0

    @pl.when(others)
    def _():
        for q in range(4):
            t_core(q).start()

    @pl.when(first)
    def _():
        for q in (2, 3):
            t_core(q, n).start()

    @pl.when(first)
    def _():
        for o in (3, 2, 1):
            t_gt(o, (zlo + o) % 4).start()
        for i in CHUNKS:
            t_pc(i).wait_recv()
            lanes = slice(m * i, n)
            pc_sum[i, :, :, lanes] = dp[i, :, core, :, lanes] + pc_in[i, :, :, lanes]
            for o in (2, 1, 3):
                t_px(i, o).start()
        for s in range(4):
            t_rc(s).wait_recv()
            rc_sum[s] = dr[s, :, core] + rc_in[s]
            for o in (2, 1, 3):
                t_rx(s, o).start()
        for i in CHUNKS:
            for o in (1, 2, 3):
                t_px(i, o).wait_recv()
            lanes = slice(m * i, n)
            pz[z, i, :, lanes] = (pc_sum[i, x, :, lanes] + px_in[0, i, :, lanes]) + (
                px_in[1, i, :, lanes] + px_in[2, i, :, lanes])
            for e in (2, 1, 3):
                t_pz(i, e, z).start()
        for s in range(4):
            for o in (1, 2, 3):
                t_rx(s, o).wait_recv()
            summed = (rc_sum[s, x] + rx_in[0, s]) + (rx_in[1, s] + rx_in[2, s])
            if s < 2:
                summed = summed + jnp.where(z == s, hess_ref[0, :, n:2 * n].astype(F32), 0.0)
            rz[z, s] = summed
            if s < 2:
                for e in (2, 1, 3):
                    t_rz(s, e, z).start()
        for e in (2, 1, 3):
            @pl.when((z + e) % 4 >= 2)
            def _(e=e):
                t_ry(e).start()

    def combine(q, _):
        t_core(q).wait_recv()
        core_sum[q] = part[q, :, core] + core_in[q]
        for o in (2, 1, 3):
            t_x(q, o).start()
        return 0

    @pl.when(others)
    def _():
        lax.fori_loop(0, 4, combine, 0)

    @pl.when(first)
    def _():
        for q in (2, 3):
            t_core(q, n).wait_recv()
            core_sum[q, :, :, n:2 * n] = part[q, :, core, :, n:2 * n] + core_in[q, :, :, n:2 * n]
            for o in (2, 1, 3):
                t_x(q, o, n).start()

    @pl.when(first)
    def _():
        for i in CHUNKS:
            for e in (1, 2, 3):
                t_pz(i, e, (z - e) % 4).wait_recv()
            lanes = slice(m * i, n)
            piv[i, x, core, :, lanes] = (pz[0, i, :, lanes] + pz[1, i, :, lanes]) + (
                pz[2, i, :, lanes] + pz[3, i, :, lanes])
            for o in (2, 1, 3):
                t_vy(i, o).start()
            for o in (3, 2, 1):
                t_vz(i, o).start()

    @pl.when((zlo == 0) & (y != 0))
    def _():
        t_gs(1, y).wait_recv()
        for o in (3, 2, 1):
            t_gt(o, (zlo + o) % 4).start()
            t_gz(o, zlo).start()

    for i in CHUNKS:
        @pl.when((zlo == 0) & (y != 0))
        def _(i=i):
            t_vy(i, 1).wait_recv()
            for o in (3, 2, 1):
                t_vz(i, o).start()

        @pl.when(zlo != 0)
        def _(i=i):
            t_vz(i, 1).wait_recv()

        for o in (2, 1, 3):
            t_vx(i, o, x).start()

    @pl.when(first)
    def _():
        for s in (0, 1):
            for e in (1, 2, 3):
                t_rz(s, e, (z - e) % 4).wait_recv()
            panel_ref[s, x, core, :, n:2 * n] = (rz[0, s] + rz[1, s]) + (rz[2, s] + rz[3, s])

        @pl.when(z >= 2)
        def _():
            for e in (1, 2, 3):
                t_ry(e).wait_recv()
            rows_ref[0, 0] = rows_ref[0, 0] + ((rz[z, z] + ry[0]) + (ry[1] + ry[2]))

        for o in (3, 2, 1):
            t_gz(o, zlo).start()

    @pl.when(zlo != 0)
    def _():
        t_gt(1, zlo).wait_recv()
        for o in (1, 2, 3):
            @pl.when((zlo + o) % 4 != 0)
            def _(o=o):
                t_gz(o, zlo).start()

    for s in (0, 1):
        @pl.when(others & (z != s))
        def _(s=s):
            got_fz(s).wait_recv()

        @pl.when(others)
        def _(s=s):
            for o in (2, 1, 3):
                t_fx(s, o, x).start()

        @pl.when(first)
        def _(s=s):
            for o in (2, 1, 3):
                t_fx(s, o, x, n).start()
    for i in CHUNKS:
        for o in (1, 2, 3):
            t_vx(i, o, (x - o) % 4).wait_recv()
        t_vc(i, core).start()

    def band_x(e, lo):
        q = (z + e) % 4
        for o in (1, 2, 3):
            t_x(q, o, lo).wait_recv()
        to = slice(lo, 2 * n)
        x_sum[q, :, to] = (core_sum[q, x, :, to] + x_in[0, q, :, to]) + (x_in[1, q, :, to] + x_in[2, q, :, to])
        if e:
            t_z(e, lo).start()

    @pl.when(others)
    def _():
        for e in (2, 1, 3):
            band_x(e, 0)

    @pl.when(first)
    def _():
        for e in ORDER:
            @pl.when((z + e) % 4 >= 2)
            def _(e=e):
                band_x(e, n)

    def spread():
        for o in (0, 1, 2, 3):
            l = (zlo - o) % 4
            if o:
                @pl.when(zlo != 0)
                def _(o=o, l=l):
                    t_gz(o, l).wait_recv()
            for v in (2, 1, 3):
                t_gy(l, v, y).start()

    def panel_core():
        for mine, lo in ((others, 0), (first, n)):
            @pl.when(mine)
            def _(lo=lo):
                for s in (0, 1):
                    for o in (1, 2, 3):
                        t_fx(s, o, (x - o) % 4, lo).wait_recv()
                    t_fc(s, core, lo).start()

    def step(k, _):
        for i in CHUNKS:
            @pl.when(k == i)
            def _(i=i):
                t_vc(i, other).wait_recv()
        factor_chunk(k, piv.at[k], inv_ref, held, done, gathered)
        for kk, work in enumerate((spread, panel_core)):
            @pl.when(k == kk)
            def _(work=work):
                work()
        return 0

    lax.fori_loop(0, 4, step, 0)
    for l in range(4):
        for o in (1, 2, 3):
            t_gy(l, o, (y - o) % 4).wait_recv()
    for mine, lo in ((others, 0), (first, n)):
        @pl.when(mine)
        def _(lo=lo):
            for s in (0, 1):
                t_fc(s, other, lo).wait_recv()

    def share_of(lo):
        for e in (1, 2, 3):
            t_z(e, lo).wait_recv()
        to = slice(lo, 2 * n)
        share_ref[:, to] = (x_sum[z, :, to] + z_in[0, :, to]) + (z_in[1, :, to] + z_in[2, :, to]) + diag_ref[:, to]

    @pl.when(others)
    def _():
        band_x(0, 0)
        share_of(0)

    @pl.when(first)
    def _():
        share_ref[...] = jnp.zeros((32, 2 * n), F32)

        @pl.when(z >= 2)
        def _():
            share_of(n)

    @pl.when(others)
    def _():
        for q in range(4):
            t_core(q).wait_send()
            for o in (1, 2, 3):
                t_x(q, o).wait_send()
        for e in (1, 2, 3):
            t_z(e).wait_send()

    @pl.when(first)
    def _():
        for q in (2, 3):
            t_core(q, n).wait_send()
            for o in (1, 2, 3):
                t_x(q, o, n).wait_send()
        for e in (1, 2, 3):
            @pl.when((z + e) % 4 >= 2)
            def _(e=e):
                t_z(e, n).wait_send()

    for mine, lo in ((others, 0), (first, n)):
        @pl.when(mine)
        def _(lo=lo):
            for s in (0, 1):
                for o in (1, 2, 3):
                    t_fx(s, o, x, lo).wait_send()
                t_fc(s, core, lo).wait_send()
    for o in (1, 2, 3):
        for l in range(4):
            t_gy(l, o, y).wait_send()

        @pl.when((zlo == 0) | ((zlo + o) % 4 != 0))
        def _(o=o):
            t_gz(o, zlo).wait_send()
    for i in CHUNKS:
        for o in (1, 2, 3):
            t_vx(i, o, x).wait_send()
        t_vc(i, core).wait_send()

    @pl.when(zlo == 0)
    def _():
        for o in (1, 2, 3):
            t_gt(o, (zlo + o) % 4).wait_send()
            for i in CHUNKS:
                t_vz(i, o).wait_send()

    @pl.when((row != 0) & (z < 2))
    def _():
        for e in (1, 2, 3):
            t_fz(e).wait_send()

    @pl.when(first)
    def _():
        for o in (1, 2, 3):
            t_gs(o, (y + o) % 4).wait_send()
            for i in CHUNKS:
                t_px(i, o).wait_send()
                t_pz(i, o, z).wait_send()
                t_vy(i, o).wait_send()
            for s in range(4):
                t_rx(s, o).wait_send()
                if s < 2:
                    t_rz(s, o, z).wait_send()

            @pl.when((z + o) % 4 >= 2)
            def _(o=o):
                t_ry(o).wait_send()
        for i in CHUNKS:
            t_pc(i).wait_send()
        for s in range(4):
            t_rc(s).wait_send()


def schur(embedded, diag, hessian):
    spec = pl.BlockSpec(memory_space=pltpu.VMEM)
    dma = pltpu.SemaphoreType.DMA
    pair = lambda *s: [dma(s), dma(s)]
    return pl.pallas_call(
        schur_kernel,
        name="schur",
        out_shape=(
            jax.ShapeDtypeStruct((512, 512), F32),
            jax.ShapeDtypeStruct((2, 4, 2, 32, 1024), F32),
            jax.ShapeDtypeStruct((4, 4, 32, 512), F32),
            jax.ShapeDtypeStruct((32, 1024), F32),
        ),
        in_specs=[spec, spec, pl.BlockSpec(memory_space=pltpu.HBM)],
        out_specs=(spec,) * 4,
        scratch_shapes=[
            VM((16, 32, 1024), BF16), dma(()),
            VM((4, 4, 2, 32, 1024), F32), VM((4, 4, 2, 16, 512), F32), VM((4, 4, 2, 32, 512), F32),
            VM((4, 4, 32, 1024), F32), VM((4, 4, 32, 1024), F32),
            VM((3, 4, 32, 1024), F32), VM((4, 32, 1024), F32), VM((3, 32, 1024), F32),
            VM((4, 4, 2, 16, 512), F32),
            VM((4, 4, 16, 512), F32), VM((4, 4, 16, 512), F32), VM((3, 4, 16, 512), F32), VM((4, 4, 16, 512), F32),
            VM((4, 4, 32, 512), F32), VM((4, 4, 32, 512), F32), VM((3, 4, 32, 512), F32), VM((4, 4, 32, 512), F32),
            VM((3, 32, 512), F32), VM((4, 4, 32, 512), F32),
            VM((4, 128, 128), F32), VM((4, 32, 128), F32), VM((128, 512), F32),
            *pair(4), *pair(4, 3), *pair(3),
            dma((3,)), dma((2,)), *pair(2, 3), *pair(2),
            dma((3,)), dma((1,)), dma((3,)), dma((1,)), *pair(3), *pair(4, 3),
            *pair(4), *pair(4, 3), *pair(4, 3), *pair(4), *pair(4, 3), *pair(2, 3), *pair(3),
            dma((4, 3)), dma((4,)), dma((4, 3)), dma((4,)), *pair(4, 3), *pair(4),
        ],
        compiler_params=pltpu.CompilerParams(
            collective_id=0, has_side_effects=True, vmem_limit_bytes=40 * 2**20
        ),
    )(embedded, diag, in_hbm(hessian))


def split(a):
    hi = a.astype(BF16)
    return hi, (a - hi.astype(F32)).astype(BF16)


def dot3(a, b, trans=False):
    dims = (((1,), (1 if trans else 0,)), ((), ()))
    mm = lambda p, q: lax.dot_general(p, q, dims, preferred_element_type=F32)
    (ah, al), (bh, bl) = a, b
    return mm(ah, bh) + (mm(ah, bl) + mm(al, bh))


def apply_kernel(inv_ref, panel_ref, rows_ref, hess_ref, share_ref, out_ref, uh, ul, vh, vl):
    row = lax.axis_index("row")
    col = lax.axis_index("col")
    at = pl.program_id(0)

    @pl.when(at == 0)
    def _():
        for lo, hi in ((0, 256), (256, 512)):
            inv = split(inv_ref[lo:hi, 0:hi])
            for j in range(4):
                part = slice(256 * j, 256 * (j + 1))
                uh[lo:hi, part], ul[lo:hi, part] = split(dot3(inv, split(panel_ref[0:hi, part])))
            for j in range(2):
                part = slice(256 * j, 256 * (j + 1))
                vh[part, lo:hi], vl[part, lo:hi] = split(dot3(split(rows_ref[part, 0:hi]), inv, trans=True))

    rows = pl.ds(pl.multiple_of(at * 128, 128), 128)
    update = dot3((vh[rows, :], vl[rows, :]), (uh[...], ul[...]))
    lane = lax.broadcasted_iota(jnp.int32, (1, 1024), 1)
    for q in range(4):
        band = at * 4 + q
        schur = hess_ref[q].astype(F32) + jnp.where(band == row, share_ref[...], 0.0)
        keep = (band * 1024 + col * 32 >= PW) & (row * 1024 + lane >= PW)
        out_ref[q] = jnp.where(keep, schur - update[32 * q:32 * (q + 1), :], 0.0)


def apply(inv, panel, rows, hessian, share):
    whole = lambda *s: pl.BlockSpec(s, lambda i: (0,) * len(s))
    return pl.pallas_call(
        apply_kernel,
        name="apply",
        grid=(4,),
        out_shape=jax.ShapeDtypeStruct((16, 32, 1024), F32),
        in_specs=[
            whole(512, 512), whole(512, 1024), whole(512, 512),
            pl.BlockSpec((4, 32, 1024), lambda i: (i, 0, 0)), whole(32, 1024),
        ],
        out_specs=pl.BlockSpec((4, 32, 1024), lambda i: (i, 0, 0)),
        scratch_shapes=[VM((512, 1024), BF16), VM((512, 1024), BF16), VM((512, 512), BF16), VM((512, 512), BF16)],
        compiler_params=pltpu.CompilerParams(
            dimension_semantics=("arbitrary",), vmem_limit_bytes=40 * 2**20
        ),
    )(inv, panel, rows, hessian, share)


def local(coupling, kinv, counts, granules, hessian, reg):
    embedded, diag = embed(coupling[0], kinv[0], counts, granules, reg)
    inv, panel, rows, share = schur(embedded, diag, hessian)
    return apply(inv, panel.reshape(512, 1024), rows.reshape(512, 512), hessian, share)


def solution(mesh):
    return jax.shard_map(
        local,
        mesh=mesh,
        in_specs=(
            P(("row", "col"), None, None),
            P(("row", "col"), None, None),
            P(("row", "col")),
            P(("row", "col"), None),
            P(None, "col", "row"),
            P("row"),
        ),
        out_specs=P(None, "col", "row"),
        check_vma=False,
    )
```

```python
import jax
import jax.numpy as jnp
from jax import lax
from jax.experimental import pallas as pl
from jax.experimental.pallas import tpu as pltpu
from jax.sharding import PartitionSpec as P

PW = 512
MESH = pl.DeviceIdType.MESH
VM = pltpu.VMEM
F32 = jnp.float32
BF16 = jnp.bfloat16
HIGH = lax.Precision.HIGHEST


def in_hbm(a):
    return pltpu.with_memory_space_constraint(a, pltpu.HBM)


def embed_kernel(
    counts_ref, granules_ref, reg_hbm, coupling_hbm, kinv_hbm, emb_ref, diag_ref,
    coupling, kinv, reg, product, loads,
):
    row = lax.axis_index("row")
    col = lax.axis_index("col")
    fetches = [
        pltpu.make_async_copy(coupling_hbm, coupling, loads.at[0]),
        pltpu.make_async_copy(kinv_hbm, kinv, loads.at[1]),
        pltpu.make_async_copy(reg_hbm, reg, loads.at[2]),
    ]
    for fetch in fetches:
        fetch.start()
    for fetch in fetches:
        fetch.wait()
    diag_at = lax.broadcasted_iota(jnp.int32, (32, 1024), 0) + col * 32
    lane_at = lax.broadcasted_iota(jnp.int32, (32, 1024), 1)
    diag_ref[...] = jnp.where(diag_at == lane_at, reg[...], 0.0)
    product[...] = jnp.dot(coupling[...], kinv[...], preferred_element_type=F32).astype(BF16)
    m, n = 128, 512
    for u in range(8):
        slot, live = jnp.int32(0), jnp.int32(0)
        for slot_of in range(8):
            here = (granules_ref[0, slot_of] == row * 8 + u) & (slot_of < counts_ref[0])
            slot = jnp.where(here, slot_of, slot)
            live = jnp.where(here, 1, live)
        block = pl.ds(pl.multiple_of(slot * m, m), m)
        shown = jnp.full((m, n), live, jnp.int32) > 0
        for which, whole in enumerate((coupling, product)):
            emb_ref[which, u * m:(u + 1) * m, :] = jnp.where(shown, whole[block, :], jnp.zeros((m, n), BF16))


def embed(coupling, kinv, counts, granules, reg):
    smem, vmem, hbm = (pl.BlockSpec(memory_space=s) for s in (pltpu.SMEM, pltpu.VMEM, pltpu.HBM))
    return pl.pallas_call(
        embed_kernel,
        name="embed",
        out_shape=(
            jax.ShapeDtypeStruct((2, 1024, 512), BF16),
            jax.ShapeDtypeStruct((32, 1024), F32),
        ),
        in_specs=[smem, smem, hbm, hbm, hbm],
        out_specs=(vmem, vmem),
        scratch_shapes=[
            VM((1024, 512), BF16), VM((512, 512), BF16), VM((1, 1024), F32), VM((1024, 512), BF16),
            pltpu.SemaphoreType.DMA((3,)),
        ],
        compiler_params=pltpu.CompilerParams(vmem_limit_bytes=32 * 2**20),
    )(counts, granules, in_hbm(reg.reshape(1, 1024)), in_hbm(coupling), in_hbm(kinv))


def dot(a, b):
    return lax.dot_general(a, b, (((1,), (0,)), ((), ())), precision=HIGH, preferred_element_type=F32)


def factor_chunk(k, chunk_ref, out, held, done, gathered):
    m, w = 128, 32
    at = pl.multiple_of(k * m, m)
    tile_at = [pl.multiple_of(((k + o) % 4) * m, m) for o in range(4)]
    for before in range(4):
        @pl.when(k == before)
        def _(before=before):
            if before:
                gathered[...] = dot(out[0:m * before, m * before:m * (before + 1)].T, out[0:m * before, :])
            else:
                gathered[...] = jnp.zeros(gathered.shape, F32)
    out[:, pl.ds(at, m)] = jnp.zeros((out.shape[0], m), F32)
    for o in range(4):
        lanes = pl.ds(tile_at[o], m)
        given = chunk_ref[:, :, :, lanes].reshape(m, m)
        held[o] = jnp.where((k + o) % 4 >= k, given, 0.0) - gathered[:, lanes]
    lane = lax.broadcasted_iota(jnp.int32, (1, m), 1)
    for j in range(4):
        tiles = [[held[o, w * j + 8 * i:w * j + 8 * i + 8, :] for o in range(4)] for i in range(4)]
        for r in range(0, w, 2):
            i0, sub = r // 8, r % 8
            one, two = lane == w * j + r, lane == w * j + r + 1
            first = i0 + (sub == 6)
            f0, f1 = (
                {i: jnp.broadcast_to(tiles[i][0][:, w * j + c:w * j + c + 1], (8, m)) for i in range(i0, 4)}
                for c in (r, r + 1)
            )
            p, q, s = f0[i0][sub:sub + 1, :], f1[i0][sub:sub + 1, :], f1[i0][sub + 1:sub + 2, :]
            det = p * s - q * q
            inverse = jnp.broadcast_to(1.0 / det, (8, m))
            top = [t[sub:sub + 1, :] for t in tiles[i0]]
            low = [t[sub + 1:sub + 2, :] for t in tiles[i0]]
            top[0] = jnp.where(one, 1.0, jnp.where(two, 0.0, top[0]))
            low[0] = jnp.where(two, 1.0, jnp.where(one, 0.0, low[0]))
            u0 = [s * t - q * l for t, l in zip(top, low)]
            u1 = [p * l - q * t for t, l in zip(top, low)]
            root0, root1 = 1.0 / jnp.sqrt(p), 1.0 / jnp.sqrt(p * det)
            for o in range(4):
                done[o, r:r + 1, :] = top[o] * root0
                done[o, r + 1:r + 2, :] = u1[o] * root1
            b0 = [jnp.broadcast_to(u, (8, m)) for u in u0]
            b1 = [jnp.broadcast_to(u, (8, m)) for u in u1]
            for i in range(first, 4):
                old = [jnp.where(one | two, 0.0, tiles[i][0])] + tiles[i][1:]
                tiles[i] = [old[o] - inverse * (f0[i] * b0[o] + f1[i] * b1[o]) for o in range(4)]
        for o in range(4):
            out[pl.ds(at + w * j, w), pl.ds(tile_at[o], m)] = done[o]
        if j < 3:
            turned = done[0].T
            gone = (lane >= w * j) & (lane < w * j + w)
            above = gone & (lane > w * j + lax.broadcasted_iota(jnp.int32, (w, 1), 0))
            wide = jnp.concatenate([jnp.where(above, 0.0, done[0])] + [done[o] for o in (1, 2, 3)], axis=1)
            cuts = (w * (j + 1), w * (j + 2), m) if j < 2 else (w * (j + 1), m)
            for lo, hi in zip(cuts, cuts[1:]):
                change = dot(turned[lo:hi], wide)
                for o in range(4):
                    old = held[o, lo:hi, :]
                    if o == 0:
                        old = jnp.where(gone, 0.0, old)
                    held[o, lo:hi, :] = old - change[:, m * o:m * (o + 1)]
    below = lane <= lax.broadcasted_iota(jnp.int32, (m, 1), 0)
    out[pl.ds(at, m), pl.ds(at, m)] = jnp.where(below, out[pl.ds(at, m), pl.ds(at, m)], 0.0)


CHUNKS = range(4)
ORDER = (2, 1, 3, 0)


def schur_kernel(
    emb_ref, diag_ref, hess_hbm,
    uh_ref, ul_ref, vh_ref, vl_ref, share_ref,
    inv_ref, panel_ref, rows_ref, hess_ref, load,
    part, dp, dr, core_in, core_sum, x_in, x_sum, z_in, piv,
    pc_in, pc_sum, px_in, pz, rc_in, rc_sum, rx_in, rz, ry, spare, held, done, gathered,
    s_core, r_core, s_x, r_x, s_z, r_z,
    s_fz, r_fz, s_fx, r_fx, s_fc, r_fc, s_gs, r_gs, s_gt, r_gt, s_gz, r_gz, s_gy, r_gy,
    s_pc, r_pc, s_px, r_px, s_pz, r_pz, s_rc, r_rc, s_rx, r_rx, s_rz, r_rz, s_ry, r_ry,
    s_vy, r_vy, s_vz, r_vz, s_vx, r_vx, s_vc, r_vc,
):
    row = lax.axis_index("row")
    col = lax.axis_index("col")
    zlo, y = row // 4, row % 4
    z, x, core = col // 8, (col // 2) % 4, col % 2
    other = 1 - core
    n, m = PW, 128
    first = row == 0

    def col_of(zz, xx, cc):
        return zz * 8 + xx * 2 + cc

    def row_of(ll, yy):
        return ll * 4 + yy

    def copy(src, dst, ss, rs, r, c):
        return pltpu.make_async_remote_copy(
            src_ref=src, dst_ref=dst, send_sem=ss, recv_sem=rs,
            device_id=(r, c), device_id_type=MESH,
        )

    def by_x(o):
        return row, col_of(z, (x + o) % 4, core)

    def by_z(e):
        return row, col_of((z + e) % 4, x, core)

    def by_y(o):
        return row_of(zlo, (y + o) % 4), col

    def by_l(o):
        return row_of((zlo + o) % 4, y), col

    pair = (row, col_of(z, x, other))

    def t_core(q, lo=0):
        return copy(part.at[q, :, other, :, lo:2 * n], core_in.at[q, :, :, lo:2 * n], s_core.at[q], r_core.at[q], *pair)

    def t_x(q, o, lo=0):
        return copy(core_sum.at[q, (x + o) % 4, :, lo:2 * n], x_in.at[o - 1, q, :, lo:2 * n], s_x.at[q, o - 1], r_x.at[q, o - 1], *by_x(o))

    def t_z(e, lo=0):
        return copy(x_sum.at[(z + e) % 4, :, lo:2 * n], z_in.at[e - 1, :, lo:2 * n], s_z.at[e - 1], r_z.at[e - 1], *by_z(e))

    def t_fz(e):
        at = panel_ref.at[z % 2, x, core]
        return copy(at, at, s_fz.at[e - 1], r_fz.at[z % 2], *by_z(e))

    def got_fz(s):
        at = panel_ref.at[s, x, core]
        return copy(at, at, s_fz.at[0], r_fz.at[s], *by_z(1))

    def t_fx(s, o, xx, lo=0):
        at = panel_ref.at[s, xx, core, :, lo:2 * n]
        return copy(at, at, s_fx.at[s, o - 1], r_fx.at[s, o - 1], *by_x(o))

    def t_fc(s, cc, lo=0):
        at = panel_ref.at[s, :, cc, :, lo:2 * n]
        return copy(at, at, s_fc.at[s], r_fc.at[s], *pair)

    def t_gs(o, yy):
        return copy(spare.at[:, yy], rows_ref.at[:, yy], s_gs.at[o - 1], r_gs.at[0], *by_y(o))

    def t_gt(o, ll):
        at = rows_ref.at[ll, y]
        return copy(at, at, s_gt.at[o - 1], r_gt.at[0], *by_l(o))

    def t_gz(o, ll):
        at = rows_ref.at[ll, y]
        return copy(at, at, s_gz.at[o - 1], r_gz.at[o - 1], *by_l(o))

    def t_gy(l, o, yy):
        at = rows_ref.at[l, yy]
        return copy(at, at, s_gy.at[l, o - 1], r_gy.at[l, o - 1], *by_y(o))

    def t_pc(i):
        return copy(dp.at[i, :, other, :, m * i:n], pc_in.at[i, :, :, m * i:n], s_pc.at[i], r_pc.at[i], *pair)

    def t_px(i, o):
        return copy(pc_sum.at[i, (x + o) % 4, :, m * i:n], px_in.at[o - 1, i, :, m * i:n],
                    s_px.at[i, o - 1], r_px.at[i, o - 1], *by_x(o))

    def t_pz(i, e, zz):
        at = pz.at[zz, i, :, m * i:n]
        return copy(at, at, s_pz.at[i, e - 1], r_pz.at[i, e - 1], *by_z(e))

    def t_vy(i, o):
        at = piv.at[i, x, core, :, m * i:n]
        return copy(at, at, s_vy.at[i, o - 1], r_vy.at[i], *by_y(o))

    def t_vz(i, o):
        at = piv.at[i, x, core, :, m * i:n]
        return copy(at, at, s_vz.at[i, o - 1], r_vz.at[i], *by_l(o))

    def t_vx(i, o, xx):
        at = piv.at[i, xx, core, :, m * i:n]
        return copy(at, at, s_vx.at[i, o - 1], r_vx.at[i, o - 1], *by_x(o))

    def t_vc(i, cc):
        at = piv.at[i, :, cc, :, m * i:n]
        return copy(at, at, s_vc.at[i], r_vc.at[i], *pair)

    def t_rc(s):
        return copy(dr.at[s, :, other], rc_in.at[s], s_rc.at[s], r_rc.at[s], *pair)

    def t_rx(s, o):
        return copy(rc_sum.at[s, (x + o) % 4], rx_in.at[o - 1, s], s_rx.at[s, o - 1], r_rx.at[s, o - 1], *by_x(o))

    def t_rz(s, e, zz):
        at = rz.at[zz, s]
        return copy(at, at, s_rz.at[s, e - 1], r_rz.at[s, e - 1], *by_z(e))

    def t_ry(e):
        return copy(rz.at[z, (z + e) % 4], ry.at[e - 1], s_ry.at[e - 1], r_ry.at[e - 1], *by_z(e))

    def outer(p, q):
        return lax.dot_general(p, q, (((1,), (1,)), ((), ())), preferred_element_type=F32)

    fetch = pltpu.make_async_copy(hess_hbm, hess_ref, load)
    fetch.start()
    barrier = pltpu.get_barrier_semaphore()

    def greet(device):
        pl.semaphore_signal(barrier, inc=1, device_id=device, device_id_type=MESH)

    greet(pair)
    for o in (1, 2, 3):
        greet(by_z(o))
        greet(by_x(o))
        greet(by_y(o))
        greet(by_l(o))

    fetch.wait()

    @pl.when(first)
    def _():
        both = outer(emb_ref[0, 0:n], emb_ref[1, 0:n]) + outer(emb_ref[1, 0:n], emb_ref[0, 0:n])
        row_block = lax.broadcasted_iota(jnp.int32, (16, 1, 1), 0)
        held_here = (hess_ref[0, :, 0:n].astype(F32) + diag_ref[:, 0:n])[None]
        both = 0.5 * both.reshape(16, 32, n) + jnp.where(row_block == col, held_here, 0.0)
        dp[...] = both.reshape(4, 4, 2, 16, n)
        dr[0:2] = outer(emb_ref[0, 0:n], emb_ref[1, n:2 * n]).reshape(2, 4, 2, 32, n)
        dr[2:4] = outer(emb_ref[1, n:2 * n], emb_ref[0, 0:n]).reshape(2, 4, 2, 32, n)
        for l in range(4):
            for yy in range(4):
                to = spare if yy else rows_ref
                to[l, yy] = hess_ref[4 * l + yy, :, 0:n].astype(F32)
        panel_ref[:, :, :, :, 0:n] = jnp.zeros((2, 4, 2, 32, n), F32)

    @pl.when((row != 0) & (z < 2))
    def _():
        panel_ref[z % 2, x, core] = hess_ref[0].astype(F32)

    def contribute(q, _):
        rows_at = pl.ds(pl.multiple_of(q * 256, 256), 256)
        part[q] = outer(emb_ref[0, rows_at], emb_ref[1]).reshape(4, 2, 32, 2 * n)
        return 0

    lax.fori_loop(0, 4, contribute, 0)
    inv_ref[...] = jnp.zeros((n, n), F32)
    pl.semaphore_wait(barrier, 13)

    @pl.when(first)
    def _():
        for i in CHUNKS:
            t_pc(i).start()
        for s in range(4):
            t_rc(s).start()
        for o in (2, 1, 3):
            t_gs(o, (y + o) % 4).start()

    @pl.when((row != 0) & (z < 2))
    def _():
        for e in (2, 1, 3):
            t_fz(e).start()

    others = row != 0

    @pl.when(others)
    def _():
        for e in ORDER:
            t_core((z + e) % 4).start()

    @pl.when(first)
    def _():
        for q in (2, 3):
            t_core(q, n).start()

    @pl.when(first)
    def _():
        for o in (3, 2, 1):
            t_gt(o, (zlo + o) % 4).start()
        for i in CHUNKS:
            t_pc(i).wait_recv()
            lanes = slice(m * i, n)
            pc_sum[i, :, :, lanes] = dp[i, :, core, :, lanes] + pc_in[i, :, :, lanes]
            for o in (2, 1, 3):
                t_px(i, o).start()
        for s in range(4):
            t_rc(s).wait_recv()
            rc_sum[s] = dr[s, :, core] + rc_in[s]
            for o in (2, 1, 3):
                t_rx(s, o).start()
        for i in CHUNKS:
            for o in (1, 2, 3):
                t_px(i, o).wait_recv()
            lanes = slice(m * i, n)
            pz[z, i, :, lanes] = (pc_sum[i, x, :, lanes] + px_in[0, i, :, lanes]) + (
                px_in[1, i, :, lanes] + px_in[2, i, :, lanes])
            for e in (2, 1, 3):
                t_pz(i, e, z).start()
        for s in range(4):
            for o in (1, 2, 3):
                t_rx(s, o).wait_recv()
            summed = (rc_sum[s, x] + rx_in[0, s]) + (rx_in[1, s] + rx_in[2, s])
            if s < 2:
                summed = summed + jnp.where(z == s, hess_ref[0, :, n:2 * n].astype(F32), 0.0)
            rz[z, s] = summed
            if s < 2:
                for e in (2, 1, 3):
                    t_rz(s, e, z).start()
        for e in (2, 1, 3):
            @pl.when((z + e) % 4 >= 2)
            def _(e=e):
                t_ry(e).start()

    def combine(q):
        t_core(q).wait_recv()
        core_sum[q] = part[q, :, core] + core_in[q]
        for o in (2, 1, 3):
            t_x(q, o).start()

    def band_x(e, lo):
        q = (z + e) % 4
        for o in (1, 2, 3):
            t_x(q, o, lo).wait_recv()
        to = slice(lo, 2 * n)
        x_sum[q, :, to] = (core_sum[q, x, :, to] + x_in[0, q, :, to]) + (x_in[1, q, :, to] + x_in[2, q, :, to])
        if e:
            t_z(e, lo).start()

    @pl.when(others)
    def _():
        for e in (2, 1):
            combine((z + e) % 4)
        for s in (0, 1):
            @pl.when(z != s)
            def _(s=s):
                got_fz(s).wait_recv()

            for o in (2, 1, 3):
                t_fx(s, o, x).start()
        for e in (3, 0):
            combine((z + e) % 4)

    @pl.when(first)
    def _():
        for q in (2, 3):
            t_core(q, n).wait_recv()
            core_sum[q, :, :, n:2 * n] = part[q, :, core, :, n:2 * n] + core_in[q, :, :, n:2 * n]
            for o in (2, 1, 3):
                t_x(q, o, n).start()

    @pl.when(first)
    def _():
        for i in CHUNKS:
            for e in (1, 2, 3):
                t_pz(i, e, (z - e) % 4).wait_recv()
            lanes = slice(m * i, n)
            piv[i, x, core, :, lanes] = (pz[0, i, :, lanes] + pz[1, i, :, lanes]) + (
                pz[2, i, :, lanes] + pz[3, i, :, lanes])
            for o in (3, 2, 1):
                t_vz(i, o).start()
            for o in (2, 1, 3):
                t_vy(i, o).start()

    @pl.when((zlo == 0) & (y != 0))
    def _():
        t_gs(1, y).wait_recv()
        for o in (3, 2, 1):
            t_gt(o, (zlo + o) % 4).start()
            t_gz(o, zlo).start()

    @pl.when(y != 0)
    def _():
        band_x(2, 0)

    for i in CHUNKS:
        @pl.when((y == 0) & (zlo != 0))
        def _(i=i):
            t_vz(i, 1).wait_recv()
            for o in (2, 1, 3):
                t_vy(i, o).start()

        @pl.when(y != 0)
        def _(i=i):
            t_vy(i, 1).wait_recv()

        for o in (2, 1, 3):
            t_vx(i, o, x).start()

    @pl.when((y == 0) & (zlo != 0))
    def _():
        for e in (2, 1, 3):
            band_x(e, 0)

    @pl.when(first)
    def _():
        for s in (0, 1):
            for e in (1, 2, 3):
                t_rz(s, e, (z - e) % 4).wait_recv()
            panel_ref[s, x, core, :, n:2 * n] = (rz[0, s] + rz[1, s]) + (rz[2, s] + rz[3, s])

        @pl.when(z >= 2)
        def _():
            for e in (1, 2, 3):
                t_ry(e).wait_recv()
            rows_ref[0, 0] = rows_ref[0, 0] + ((rz[z, z] + ry[0]) + (ry[1] + ry[2]))

        for o in (3, 2, 1):
            t_gz(o, zlo).start()

    @pl.when(zlo != 0)
    def _():
        t_gt(1, zlo).wait_recv()
        for o in (1, 2, 3):
            @pl.when((zlo + o) % 4 != 0)
            def _(o=o):
                t_gz(o, zlo).start()

    @pl.when(first)
    def _():
        for s in (0, 1):
            for o in (2, 1, 3):
                t_fx(s, o, x, n).start()

    @pl.when(y != 0)
    def _():
        for e in (1, 3):
            band_x(e, 0)

    for i in CHUNKS:
        for o in (1, 2, 3):
            t_vx(i, o, (x - o) % 4).wait_recv()
        t_vc(i, core).start()

    @pl.when(first)
    def _():
        for e in ORDER:
            @pl.when((z + e) % 4 >= 2)
            def _(e=e):
                band_x(e, n)

    def spread():
        for o in (0, 1, 2, 3):
            l = (zlo - o) % 4
            if o:
                @pl.when(zlo != 0)
                def _(o=o, l=l):
                    t_gz(o, l).wait_recv()
            for v in (2, 1, 3):
                t_gy(l, v, y).start()

    def panel_core(lo):
        for s in (0, 1):
            for o in (1, 2, 3):
                t_fx(s, o, (x - o) % 4, lo).wait_recv()
            t_fc(s, core, lo).start()

    @pl.when(others)
    def _():
        panel_core(0)

    def late_panel():
        @pl.when(first)
        def _():
            panel_core(n)

    def step(k, _):
        for i in CHUNKS:
            @pl.when(k == i)
            def _(i=i):
                t_vc(i, other).wait_recv()
        factor_chunk(k, piv.at[k], inv_ref, held, done, gathered)
        for kk, work in enumerate((spread, late_panel)):
            @pl.when(k == kk)
            def _(work=work):
                work()
        return 0

    lax.fori_loop(0, 4, step, 0)
    for l in range(4):
        for o in (1, 2, 3):
            t_gy(l, o, (y - o) % 4).wait_recv()
    for mine, lo in ((others, 0), (first, n)):
        @pl.when(mine)
        def _(lo=lo):
            for s in (0, 1):
                t_fc(s, other, lo).wait_recv()

    for lo, hi in ((0, 256), (256, 512)):
        inv = split(inv_ref[lo:hi, 0:hi])
        for j in range(4):
            to = slice(256 * j, 256 * (j + 1))
            given = panel_ref[:, :, :, :, to].reshape(n, 256)
            uh_ref[lo:hi, to], ul_ref[lo:hi, to] = split(dot3(inv, split(given[0:hi])))
        for j in range(2):
            to = slice(256 * j, 256 * (j + 1))
            given = rows_ref[2 * j:2 * j + 2].reshape(256, n)
            vh_ref[to, lo:hi], vl_ref[to, lo:hi] = split(dot3(split(given[:, 0:hi]), inv, trans=True))

    def share_of(lo):
        for e in (1, 2, 3):
            t_z(e, lo).wait_recv()
        to = slice(lo, 2 * n)
        share_ref[:, to] = (x_sum[z, :, to] + z_in[0, :, to]) + (z_in[1, :, to] + z_in[2, :, to]) + diag_ref[:, to]

    @pl.when(others)
    def _():
        band_x(0, 0)
        share_of(0)

    @pl.when(first)
    def _():
        share_ref[...] = jnp.zeros((32, 2 * n), F32)

        @pl.when(z >= 2)
        def _():
            share_of(n)

    @pl.when(others)
    def _():
        for q in range(4):
            t_core(q).wait_send()
            for o in (1, 2, 3):
                t_x(q, o).wait_send()
        for e in (1, 2, 3):
            t_z(e).wait_send()

    @pl.when(first)
    def _():
        for q in (2, 3):
            t_core(q, n).wait_send()
            for o in (1, 2, 3):
                t_x(q, o, n).wait_send()
        for e in (1, 2, 3):
            @pl.when((z + e) % 4 >= 2)
            def _(e=e):
                t_z(e, n).wait_send()

    for mine, lo in ((others, 0), (first, n)):
        @pl.when(mine)
        def _(lo=lo):
            for s in (0, 1):
                for o in (1, 2, 3):
                    t_fx(s, o, x, lo).wait_send()
                t_fc(s, core, lo).wait_send()
    for o in (1, 2, 3):
        for l in range(4):
            t_gy(l, o, y).wait_send()

        @pl.when((zlo == 0) | ((zlo + o) % 4 != 0))
        def _(o=o):
            t_gz(o, zlo).wait_send()
    for i in CHUNKS:
        for o in (1, 2, 3):
            t_vx(i, o, x).wait_send()
        t_vc(i, core).wait_send()

    @pl.when(zlo == 0)
    def _():
        for o in (1, 2, 3):
            t_gt(o, (zlo + o) % 4).wait_send()

    @pl.when(y == 0)
    def _():
        for i in CHUNKS:
            for o in (1, 2, 3):
                t_vy(i, o).wait_send()

    @pl.when((row != 0) & (z < 2))
    def _():
        for e in (1, 2, 3):
            t_fz(e).wait_send()

    @pl.when(first)
    def _():
        for o in (1, 2, 3):
            t_gs(o, (y + o) % 4).wait_send()
            for i in CHUNKS:
                t_px(i, o).wait_send()
                t_pz(i, o, z).wait_send()
                t_vz(i, o).wait_send()
            for s in range(4):
                t_rx(s, o).wait_send()
                if s < 2:
                    t_rz(s, o, z).wait_send()

            @pl.when((z + o) % 4 >= 2)
            def _(o=o):
                t_ry(o).wait_send()
        for i in CHUNKS:
            t_pc(i).wait_send()
        for s in range(4):
            t_rc(s).wait_send()


def schur(embedded, diag, hessian):
    spec = pl.BlockSpec(memory_space=pltpu.VMEM)
    dma = pltpu.SemaphoreType.DMA
    pair = lambda *s: [dma(s), dma(s)]
    return pl.pallas_call(
        schur_kernel,
        name="schur",
        out_shape=(
            jax.ShapeDtypeStruct((512, 1024), BF16), jax.ShapeDtypeStruct((512, 1024), BF16),
            jax.ShapeDtypeStruct((512, 512), BF16), jax.ShapeDtypeStruct((512, 512), BF16),
            jax.ShapeDtypeStruct((32, 1024), F32),
        ),
        in_specs=[spec, spec, pl.BlockSpec(memory_space=pltpu.HBM)],
        out_specs=(spec,) * 5,
        scratch_shapes=[
            VM((512, 512), F32), VM((2, 4, 2, 32, 1024), F32), VM((4, 4, 32, 512), F32),
            VM((16, 32, 1024), BF16), dma(()),
            VM((4, 4, 2, 32, 1024), F32), VM((4, 4, 2, 16, 512), F32), VM((4, 4, 2, 32, 512), F32),
            VM((4, 4, 32, 1024), F32), VM((4, 4, 32, 1024), F32),
            VM((3, 4, 32, 1024), F32), VM((4, 32, 1024), F32), VM((3, 32, 1024), F32),
            VM((4, 4, 2, 16, 512), F32),
            VM((4, 4, 16, 512), F32), VM((4, 4, 16, 512), F32), VM((3, 4, 16, 512), F32), VM((4, 4, 16, 512), F32),
            VM((4, 4, 32, 512), F32), VM((4, 4, 32, 512), F32), VM((3, 4, 32, 512), F32), VM((4, 4, 32, 512), F32),
            VM((3, 32, 512), F32), VM((4, 4, 32, 512), F32),
            VM((4, 128, 128), F32), VM((4, 32, 128), F32), VM((128, 512), F32),
            *pair(4), *pair(4, 3), *pair(3),
            dma((3,)), dma((2,)), *pair(2, 3), *pair(2),
            dma((3,)), dma((1,)), dma((3,)), dma((1,)), *pair(3), *pair(4, 3),
            *pair(4), *pair(4, 3), *pair(4, 3), *pair(4), *pair(4, 3), *pair(2, 3), *pair(3),
            dma((4, 3)), dma((4,)), dma((4, 3)), dma((4,)), *pair(4, 3), *pair(4),
        ],
        compiler_params=pltpu.CompilerParams(
            collective_id=0, has_side_effects=True, vmem_limit_bytes=40 * 2**20
        ),
    )(embedded, diag, in_hbm(hessian))


def split(a):
    hi = a.astype(BF16)
    return hi, (a - hi.astype(F32)).astype(BF16)


def dot3(a, b, trans=False):
    dims = (((1,), (1 if trans else 0,)), ((), ()))
    mm = lambda p, q: lax.dot_general(p, q, dims, preferred_element_type=F32)
    (ah, al), (bh, bl) = a, b
    return mm(ah, bh) + (mm(ah, bl) + mm(al, bh))


def apply_kernel(uh, ul, vh, vl, hess_ref, share_ref, out_ref):
    row = lax.axis_index("row")
    col = lax.axis_index("col")
    at = pl.program_id(0)
    rows = pl.ds(pl.multiple_of(at * 128, 128), 128)
    update = dot3((vh[rows, :], vl[rows, :]), (uh[...], ul[...]))
    lane = lax.broadcasted_iota(jnp.int32, (1, 1024), 1)
    for q in range(4):
        band = at * 4 + q
        schur = hess_ref[q].astype(F32) + jnp.where(band == row, share_ref[...], 0.0)
        keep = (band * 1024 + col * 32 >= PW) & (row * 1024 + lane >= PW)
        out_ref[q] = jnp.where(keep, schur - update[32 * q:32 * (q + 1), :], 0.0)


def apply(uh, ul, vh, vl, hessian, share):
    whole = lambda *s: pl.BlockSpec(s, lambda i: (0,) * len(s))
    return pl.pallas_call(
        apply_kernel,
        name="apply",
        grid=(4,),
        out_shape=jax.ShapeDtypeStruct((16, 32, 1024), F32),
        in_specs=[
            whole(512, 1024), whole(512, 1024), whole(512, 512), whole(512, 512),
            pl.BlockSpec((4, 32, 1024), lambda i: (i, 0, 0)), whole(32, 1024),
        ],
        out_specs=pl.BlockSpec((4, 32, 1024), lambda i: (i, 0, 0)),
        compiler_params=pltpu.CompilerParams(
            dimension_semantics=("arbitrary",), vmem_limit_bytes=40 * 2**20
        ),
    )(uh, ul, vh, vl, hessian, share)


def local(coupling, kinv, counts, granules, hessian, reg):
    embedded, diag = embed(coupling[0], kinv[0], counts, granules, reg)
    uh, ul, vh, vl, share = schur(embedded, diag, hessian)
    return apply(uh, ul, vh, vl, hessian, share)


def solution(mesh):
    return jax.shard_map(
        local,
        mesh=mesh,
        in_specs=(
            P(("row", "col"), None, None),
            P(("row", "col"), None, None),
            P(("row", "col")),
            P(("row", "col"), None),
            P(None, "col", "row"),
            P("row"),
        ),
        out_specs=P(None, "col", "row"),
        check_vma=False,
    )
```

```python
import jax
import jax.numpy as jnp
from jax import lax
from jax.experimental import pallas as pl
from jax.experimental.pallas import tpu as pltpu
from jax.sharding import PartitionSpec as P

PW = 512
MESH = pl.DeviceIdType.MESH
VM = pltpu.VMEM
F32 = jnp.float32
BF16 = jnp.bfloat16
HIGH = lax.Precision.HIGHEST


def in_hbm(a):
    return pltpu.with_memory_space_constraint(a, pltpu.HBM)


def embed_kernel(
    counts_ref, granules_ref, reg_hbm, coupling_hbm, kinv_hbm, emb_ref, diag_ref,
    coupling, kinv, reg, product, loads,
):
    row = lax.axis_index("row")
    col = lax.axis_index("col")
    fetches = [
        pltpu.make_async_copy(coupling_hbm, coupling, loads.at[0]),
        pltpu.make_async_copy(kinv_hbm, kinv, loads.at[1]),
        pltpu.make_async_copy(reg_hbm, reg, loads.at[2]),
    ]
    for fetch in fetches:
        fetch.start()
    for fetch in fetches:
        fetch.wait()
    diag_at = lax.broadcasted_iota(jnp.int32, (32, 1024), 0) + col * 32
    lane_at = lax.broadcasted_iota(jnp.int32, (32, 1024), 1)
    diag_ref[...] = jnp.where(diag_at == lane_at, reg[...], 0.0)
    product[...] = jnp.dot(coupling[...], kinv[...], preferred_element_type=F32).astype(BF16)
    m, n = 128, 512
    for u in range(8):
        slot, live = jnp.int32(0), jnp.int32(0)
        for slot_of in range(8):
            here = (granules_ref[0, slot_of] == row * 8 + u) & (slot_of < counts_ref[0])
            slot = jnp.where(here, slot_of, slot)
            live = jnp.where(here, 1, live)
        block = pl.ds(pl.multiple_of(slot * m, m), m)
        shown = jnp.full((m, n), live, jnp.int32) > 0
        for which, whole in enumerate((coupling, product)):
            emb_ref[which, u * m:(u + 1) * m, :] = jnp.where(shown, whole[block, :], jnp.zeros((m, n), BF16))


def embed(coupling, kinv, counts, granules, reg):
    smem, vmem, hbm = (pl.BlockSpec(memory_space=s) for s in (pltpu.SMEM, pltpu.VMEM, pltpu.HBM))
    return pl.pallas_call(
        embed_kernel,
        name="embed",
        out_shape=(
            jax.ShapeDtypeStruct((2, 1024, 512), BF16),
            jax.ShapeDtypeStruct((32, 1024), F32),
        ),
        in_specs=[smem, smem, hbm, hbm, hbm],
        out_specs=(vmem, vmem),
        scratch_shapes=[
            VM((1024, 512), BF16), VM((512, 512), BF16), VM((1, 1024), F32), VM((1024, 512), BF16),
            pltpu.SemaphoreType.DMA((3,)),
        ],
        compiler_params=pltpu.CompilerParams(vmem_limit_bytes=32 * 2**20),
    )(counts, granules, in_hbm(reg.reshape(1, 1024)), in_hbm(coupling), in_hbm(kinv))


def dot(a, b):
    return lax.dot_general(a, b, (((1,), (0,)), ((), ())), precision=HIGH, preferred_element_type=F32)


def factor_chunk(k, chunk_ref, out, held, done, gathered):
    m, w = 128, 32
    at = pl.multiple_of(k * m, m)
    tile_at = [pl.multiple_of(((k + o) % 4) * m, m) for o in range(4)]
    for before in range(4):
        @pl.when(k == before)
        def _(before=before):
            if before:
                gathered[...] = dot(out[0:m * before, m * before:m * (before + 1)].T, out[0:m * before, :])
            else:
                gathered[...] = jnp.zeros(gathered.shape, F32)
    out[:, pl.ds(at, m)] = jnp.zeros((out.shape[0], m), F32)
    for o in range(4):
        lanes = pl.ds(tile_at[o], m)
        given = chunk_ref[:, :, :, lanes].reshape(m, m)
        held[o] = jnp.where((k + o) % 4 >= k, given, 0.0) - gathered[:, lanes]
    lane = lax.broadcasted_iota(jnp.int32, (1, m), 1)
    for j in range(4):
        tiles = [[held[o, w * j + 8 * i:w * j + 8 * i + 8, :] for o in range(4)] for i in range(4)]
        for r in range(0, w, 2):
            i0, sub = r // 8, r % 8
            one, two = lane == w * j + r, lane == w * j + r + 1
            first = i0 + (sub == 6)
            f0, f1 = (
                {i: jnp.broadcast_to(tiles[i][0][:, w * j + c:w * j + c + 1], (8, m)) for i in range(i0, 4)}
                for c in (r, r + 1)
            )
            p, q, s = f0[i0][sub:sub + 1, :], f1[i0][sub:sub + 1, :], f1[i0][sub + 1:sub + 2, :]
            det = p * s - q * q
            inverse = jnp.broadcast_to(1.0 / det, (8, m))
            top = [t[sub:sub + 1, :] for t in tiles[i0]]
            low = [t[sub + 1:sub + 2, :] for t in tiles[i0]]
            top[0] = jnp.where(one, 1.0, jnp.where(two, 0.0, top[0]))
            low[0] = jnp.where(two, 1.0, jnp.where(one, 0.0, low[0]))
            u0 = [s * t - q * l for t, l in zip(top, low)]
            u1 = [p * l - q * t for t, l in zip(top, low)]
            root0, root1 = 1.0 / jnp.sqrt(p), 1.0 / jnp.sqrt(p * det)
            for o in range(4):
                done[o, r:r + 1, :] = top[o] * root0
                done[o, r + 1:r + 2, :] = u1[o] * root1
            b0 = [jnp.broadcast_to(u, (8, m)) for u in u0]
            b1 = [jnp.broadcast_to(u, (8, m)) for u in u1]
            for i in range(first, 4):
                old = [jnp.where(one | two, 0.0, tiles[i][0])] + tiles[i][1:]
                tiles[i] = [old[o] - inverse * (f0[i] * b0[o] + f1[i] * b1[o]) for o in range(4)]
        for o in range(4):
            out[pl.ds(at + w * j, w), pl.ds(tile_at[o], m)] = done[o]
        if j < 3:
            turned = done[0].T
            gone = (lane >= w * j) & (lane < w * j + w)
            above = gone & (lane > w * j + lax.broadcasted_iota(jnp.int32, (w, 1), 0))
            wide = jnp.concatenate([jnp.where(above, 0.0, done[0])] + [done[o] for o in (1, 2, 3)], axis=1)
            cuts = (w * (j + 1), w * (j + 2), m) if j < 2 else (w * (j + 1), m)
            for lo, hi in zip(cuts, cuts[1:]):
                change = dot(turned[lo:hi], wide)
                for o in range(4):
                    old = held[o, lo:hi, :]
                    if o == 0:
                        old = jnp.where(gone, 0.0, old)
                    held[o, lo:hi, :] = old - change[:, m * o:m * (o + 1)]
    below = lane <= lax.broadcasted_iota(jnp.int32, (m, 1), 0)
    out[pl.ds(at, m), pl.ds(at, m)] = jnp.where(below, out[pl.ds(at, m), pl.ds(at, m)], 0.0)


CHUNKS = range(4)
ORDER = (2, 1, 3, 0)


def schur_kernel(
    emb_ref, diag_ref, hess_hbm,
    uh_ref, ul_ref, vh_ref, vl_ref, share_ref,
    inv_ref, panel_ref, rows_ref, hess_ref, load,
    part, dp, dr, core_in, core_sum, x_in, x_sum, z_in, piv,
    pc_in, pc_sum, px_in, pz, rc_in, rc_sum, rx_in, rz, ry, spare, held, done, gathered,
    s_core, r_core, s_x, r_x, s_z, r_z,
    s_fz, r_fz, s_fx, r_fx, s_fc, r_fc, s_gs, r_gs, s_gt, r_gt, s_gz, r_gz, s_gy, r_gy,
    s_pc, r_pc, s_px, r_px, s_pz, r_pz, s_rc, r_rc, s_rx, r_rx, s_rz, r_rz, s_ry, r_ry,
    s_vy, r_vy, s_vz, r_vz, s_vx, r_vx, s_vc, r_vc,
):
    row = lax.axis_index("row")
    col = lax.axis_index("col")
    zlo, y = row // 4, row % 4
    z, x, core = col // 8, (col // 2) % 4, col % 2
    other = 1 - core
    n, m = PW, 128
    first = row == 0

    def col_of(zz, xx, cc):
        return zz * 8 + xx * 2 + cc

    def row_of(ll, yy):
        return ll * 4 + yy

    def copy(src, dst, ss, rs, r, c):
        return pltpu.make_async_remote_copy(
            src_ref=src, dst_ref=dst, send_sem=ss, recv_sem=rs,
            device_id=(r, c), device_id_type=MESH,
        )

    def by_x(o):
        return row, col_of(z, (x + o) % 4, core)

    def by_z(e):
        return row, col_of((z + e) % 4, x, core)

    def by_y(o):
        return row_of(zlo, (y + o) % 4), col

    def by_l(o):
        return row_of((zlo + o) % 4, y), col

    pair = (row, col_of(z, x, other))

    def t_core(q, lo=0):
        return copy(part.at[q, :, other, :, lo:2 * n], core_in.at[q, :, :, lo:2 * n], s_core.at[q], r_core.at[q], *pair)

    def t_x(q, o, lo=0):
        return copy(core_sum.at[q, (x + o) % 4, :, lo:2 * n], x_in.at[o - 1, q, :, lo:2 * n], s_x.at[q, o - 1], r_x.at[q, o - 1], *by_x(o))

    def t_z(e, lo=0):
        return copy(x_sum.at[(z + e) % 4, :, lo:2 * n], z_in.at[e - 1, :, lo:2 * n], s_z.at[e - 1], r_z.at[e - 1], *by_z(e))

    def t_fz(e):
        at = panel_ref.at[z % 2, x, core]
        return copy(at, at, s_fz.at[e - 1], r_fz.at[z % 2], *by_z(e))

    def got_fz(s):
        at = panel_ref.at[s, x, core]
        return copy(at, at, s_fz.at[0], r_fz.at[s], *by_z(1))

    def t_fx(s, o, xx, lo=0):
        at = panel_ref.at[s, xx, core, :, lo:2 * n]
        return copy(at, at, s_fx.at[s, o - 1], r_fx.at[s, o - 1], *by_x(o))

    def t_fc(s, cc, lo=0):
        at = panel_ref.at[s, :, cc, :, lo:2 * n]
        return copy(at, at, s_fc.at[s], r_fc.at[s], *pair)

    def t_gs(o, yy):
        return copy(spare.at[:, yy], rows_ref.at[:, yy], s_gs.at[o - 1], r_gs.at[0], *by_y(o))

    def t_gt(o, ll):
        at = rows_ref.at[ll, y]
        return copy(at, at, s_gt.at[o - 1], r_gt.at[0], *by_l(o))

    def t_gz(o, ll):
        at = rows_ref.at[ll, y]
        return copy(at, at, s_gz.at[o - 1], r_gz.at[o - 1], *by_l(o))

    def t_gy(l, o, yy):
        at = rows_ref.at[l, yy]
        return copy(at, at, s_gy.at[l, o - 1], r_gy.at[l, o - 1], *by_y(o))

    def t_pc(i):
        return copy(dp.at[i, :, other, :, m * i:n], pc_in.at[i, :, :, m * i:n], s_pc.at[i], r_pc.at[i], *pair)

    def t_px(i, o):
        return copy(pc_sum.at[i, (x + o) % 4, :, m * i:n], px_in.at[o - 1, i, :, m * i:n],
                    s_px.at[i, o - 1], r_px.at[i, o - 1], *by_x(o))

    def t_pz(i, e, zz):
        at = pz.at[zz, i, :, m * i:n]
        return copy(at, at, s_pz.at[i, e - 1], r_pz.at[i, e - 1], *by_z(e))

    def t_vy(i, o):
        at = piv.at[i, x, core, :, m * i:n]
        return copy(at, at, s_vy.at[i, o - 1], r_vy.at[i], *by_y(o))

    def t_vz(i, o):
        at = piv.at[i, x, core, :, m * i:n]
        return copy(at, at, s_vz.at[i, o - 1], r_vz.at[i], *by_l(o))

    def t_vx(i, o, xx):
        at = piv.at[i, xx, core, :, m * i:n]
        return copy(at, at, s_vx.at[i, o - 1], r_vx.at[i, o - 1], *by_x(o))

    def t_vc(i, cc):
        at = piv.at[i, :, cc, :, m * i:n]
        return copy(at, at, s_vc.at[i], r_vc.at[i], *pair)

    def t_rc(s):
        return copy(dr.at[s, :, other], rc_in.at[s], s_rc.at[s], r_rc.at[s], *pair)

    def t_rx(s, o):
        return copy(rc_sum.at[s, (x + o) % 4], rx_in.at[o - 1, s], s_rx.at[s, o - 1], r_rx.at[s, o - 1], *by_x(o))

    def t_rz(s, e, zz):
        at = rz.at[zz, s]
        return copy(at, at, s_rz.at[s, e - 1], r_rz.at[s, e - 1], *by_z(e))

    def t_ry(e):
        return copy(rz.at[z, (z + e) % 4], ry.at[e - 1], s_ry.at[e - 1], r_ry.at[e - 1], *by_z(e))

    def outer(p, q):
        return lax.dot_general(p, q, (((1,), (1,)), ((), ())), preferred_element_type=F32)

    fetch = pltpu.make_async_copy(hess_hbm, hess_ref, load)
    fetch.start()
    barrier = pltpu.get_barrier_semaphore()

    def greet(device):
        pl.semaphore_signal(barrier, inc=1, device_id=device, device_id_type=MESH)

    greet(pair)
    for o in (1, 2, 3):
        greet(by_z(o))
        greet(by_x(o))
        greet(by_y(o))
        greet(by_l(o))

    fetch.wait()

    @pl.when(first)
    def _():
        both = outer(emb_ref[0, 0:n], emb_ref[1, 0:n]) + outer(emb_ref[1, 0:n], emb_ref[0, 0:n])
        row_block = lax.broadcasted_iota(jnp.int32, (16, 1, 1), 0)
        held_here = (hess_ref[0, :, 0:n].astype(F32) + diag_ref[:, 0:n])[None]
        both = 0.5 * both.reshape(16, 32, n) + jnp.where(row_block == col, held_here, 0.0)
        dp[...] = both.reshape(4, 4, 2, 16, n)
        dr[0:2] = outer(emb_ref[0, 0:n], emb_ref[1, n:2 * n]).reshape(2, 4, 2, 32, n)
        dr[2:4] = outer(emb_ref[1, n:2 * n], emb_ref[0, 0:n]).reshape(2, 4, 2, 32, n)
        for l in range(4):
            for yy in range(4):
                to = spare if yy else rows_ref
                to[l, yy] = hess_ref[4 * l + yy, :, 0:n].astype(F32)
        panel_ref[:, :, :, :, 0:n] = jnp.zeros((2, 4, 2, 32, n), F32)

    @pl.when((row != 0) & (z < 2))
    def _():
        panel_ref[z % 2, x, core] = hess_ref[0].astype(F32)

    def contribute(q, _):
        rows_at = pl.ds(pl.multiple_of(q * 256, 256), 256)
        part[q] = outer(emb_ref[0, rows_at], emb_ref[1]).reshape(4, 2, 32, 2 * n)
        return 0

    lax.fori_loop(0, 4, contribute, 0)
    inv_ref[...] = jnp.zeros((n, n), F32)
    pl.semaphore_wait(barrier, 13)

    @pl.when(first)
    def _():
        for i in CHUNKS:
            t_pc(i).start()
        for s in range(4):
            t_rc(s).start()
        for o in (2, 1, 3):
            t_gs(o, (y + o) % 4).start()

    @pl.when((row != 0) & (z < 2))
    def _():
        for e in (2, 1, 3):
            t_fz(e).start()

    others = row != 0

    @pl.when(others)
    def _():
        for q in range(4):
            t_core(q).start()

    @pl.when(first)
    def _():
        for q in (2, 3):
            t_core(q, n).start()

    @pl.when(first)
    def _():
        for o in (3, 2, 1):
            t_gt(o, (zlo + o) % 4).start()
        for i in CHUNKS:
            t_pc(i).wait_recv()
            lanes = slice(m * i, n)
            pc_sum[i, :, :, lanes] = dp[i, :, core, :, lanes] + pc_in[i, :, :, lanes]
            for o in (2, 1, 3):
                t_px(i, o).start()
        for s in range(4):
            t_rc(s).wait_recv()
            rc_sum[s] = dr[s, :, core] + rc_in[s]
            for o in (2, 1, 3):
                t_rx(s, o).start()
        for i in CHUNKS:
            for o in (1, 2, 3):
                t_px(i, o).wait_recv()
            lanes = slice(m * i, n)
            pz[z, i, :, lanes] = (pc_sum[i, x, :, lanes] + px_in[0, i, :, lanes]) + (
                px_in[1, i, :, lanes] + px_in[2, i, :, lanes])
            for e in (2, 1, 3):
                t_pz(i, e, z).start()
        for s in range(4):
            for o in (1, 2, 3):
                t_rx(s, o).wait_recv()
            summed = (rc_sum[s, x] + rx_in[0, s]) + (rx_in[1, s] + rx_in[2, s])
            if s < 2:
                summed = summed + jnp.where(z == s, hess_ref[0, :, n:2 * n].astype(F32), 0.0)
            rz[z, s] = summed
            if s < 2:
                for e in (2, 1, 3):
                    t_rz(s, e, z).start()
        for e in (2, 1, 3):
            @pl.when((z + e) % 4 >= 2)
            def _(e=e):
                t_ry(e).start()

    def combine(q):
        t_core(q).wait_recv()
        core_sum[q] = part[q, :, core] + core_in[q]
        for o in (2, 1, 3):
            t_x(q, o).start()

    @pl.when(others)
    def _():
        for q in (0, 1):
            combine(q)
        for s in (0, 1):
            @pl.when(z != s)
            def _(s=s):
                got_fz(s).wait_recv()

            for o in (2, 1, 3):
                t_fx(s, o, x).start()
        for q in (2, 3):
            combine(q)

    @pl.when(first)
    def _():
        for q in (2, 3):
            t_core(q, n).wait_recv()
            core_sum[q, :, :, n:2 * n] = part[q, :, core, :, n:2 * n] + core_in[q, :, :, n:2 * n]
            for o in (2, 1, 3):
                t_x(q, o, n).start()

    @pl.when(first)
    def _():
        for i in CHUNKS:
            for e in (1, 2, 3):
                t_pz(i, e, (z - e) % 4).wait_recv()
            lanes = slice(m * i, n)
            piv[i, x, core, :, lanes] = (pz[0, i, :, lanes] + pz[1, i, :, lanes]) + (
                pz[2, i, :, lanes] + pz[3, i, :, lanes])
            for o in (2, 1, 3):
                t_vy(i, o).start()
            for o in (3, 2, 1):
                t_vz(i, o).start()

    @pl.when((zlo == 0) & (y != 0))
    def _():
        t_gs(1, y).wait_recv()
        for o in (3, 2, 1):
            t_gt(o, (zlo + o) % 4).start()
            t_gz(o, zlo).start()

    for i in CHUNKS:
        @pl.when((zlo == 0) & (y != 0))
        def _(i=i):
            t_vy(i, 1).wait_recv()
            for o in (3, 2, 1):
                t_vz(i, o).start()

        @pl.when(zlo != 0)
        def _(i=i):
            t_vz(i, 1).wait_recv()

        for o in (2, 1, 3):
            t_vx(i, o, x).start()

    @pl.when(first)
    def _():
        for s in (0, 1):
            for e in (1, 2, 3):
                t_rz(s, e, (z - e) % 4).wait_recv()
            panel_ref[s, x, core, :, n:2 * n] = (rz[0, s] + rz[1, s]) + (rz[2, s] + rz[3, s])

        @pl.when(z >= 2)
        def _():
            for e in (1, 2, 3):
                t_ry(e).wait_recv()
            rows_ref[0, 0] = rows_ref[0, 0] + ((rz[z, z] + ry[0]) + (ry[1] + ry[2]))

        for o in (3, 2, 1):
            t_gz(o, zlo).start()

    @pl.when(zlo != 0)
    def _():
        t_gt(1, zlo).wait_recv()
        for o in (1, 2, 3):
            @pl.when((zlo + o) % 4 != 0)
            def _(o=o):
                t_gz(o, zlo).start()

    @pl.when(first)
    def _():
        for s in (0, 1):
            for o in (2, 1, 3):
                t_fx(s, o, x, n).start()

    for i in CHUNKS:
        for o in (1, 2, 3):
            t_vx(i, o, (x - o) % 4).wait_recv()
        t_vc(i, core).start()

    def band_x(e, lo):
        q = (z + e) % 4
        for o in (1, 2, 3):
            t_x(q, o, lo).wait_recv()
        to = slice(lo, 2 * n)
        x_sum[q, :, to] = (core_sum[q, x, :, to] + x_in[0, q, :, to]) + (x_in[1, q, :, to] + x_in[2, q, :, to])
        if e:
            t_z(e, lo).start()

    @pl.when(others)
    def _():
        for e in (2, 1, 3):
            band_x(e, 0)

    @pl.when(first)
    def _():
        for e in ORDER:
            @pl.when((z + e) % 4 >= 2)
            def _(e=e):
                band_x(e, n)

    def spread():
        for o in (0, 1, 2, 3):
            l = (zlo - o) % 4
            if o:
                @pl.when(zlo != 0)
                def _(o=o, l=l):
                    t_gz(o, l).wait_recv()
            for v in (2, 1, 3):
                t_gy(l, v, y).start()

    def panel_core():
        for mine, lo in ((others, 0), (first, n)):
            @pl.when(mine)
            def _(lo=lo):
                for s in (0, 1):
                    for o in (1, 2, 3):
                        t_fx(s, o, (x - o) % 4, lo).wait_recv()
                    t_fc(s, core, lo).start()

    def step(k, _):
        for i in CHUNKS:
            @pl.when(k == i)
            def _(i=i):
                t_vc(i, other).wait_recv()
        factor_chunk(k, piv.at[k], inv_ref, held, done, gathered)
        for kk, work in enumerate((spread, panel_core)):
            @pl.when(k == kk)
            def _(work=work):
                work()
        return 0

    lax.fori_loop(0, 4, step, 0)
    for l in range(4):
        for o in (1, 2, 3):
            t_gy(l, o, (y - o) % 4).wait_recv()
    for mine, lo in ((others, 0), (first, n)):
        @pl.when(mine)
        def _(lo=lo):
            for s in (0, 1):
                t_fc(s, other, lo).wait_recv()

    for lo, hi in ((0, 256), (256, 512)):
        inv = split(inv_ref[lo:hi, 0:hi])
        for j in range(4):
            to = slice(256 * j, 256 * (j + 1))
            given = panel_ref[:, :, :, :, to].reshape(n, 256)
            uh_ref[lo:hi, to], ul_ref[lo:hi, to] = split(dot3(inv, split(given[0:hi])))
        for j in range(2):
            to = slice(256 * j, 256 * (j + 1))
            given = rows_ref[2 * j:2 * j + 2].reshape(256, n)
            vh_ref[to, lo:hi], vl_ref[to, lo:hi] = split(dot3(split(given[:, 0:hi]), inv, trans=True))

    def share_of(lo):
        for e in (1, 2, 3):
            t_z(e, lo).wait_recv()
        to = slice(lo, 2 * n)
        share_ref[:, to] = (x_sum[z, :, to] + z_in[0, :, to]) + (z_in[1, :, to] + z_in[2, :, to]) + diag_ref[:, to]

    @pl.when(others)
    def _():
        band_x(0, 0)
        share_of(0)

    @pl.when(first)
    def _():
        share_ref[...] = jnp.zeros((32, 2 * n), F32)

        @pl.when(z >= 2)
        def _():
            share_of(n)

    @pl.when(others)
    def _():
        for q in range(4):
            t_core(q).wait_send()
            for o in (1, 2, 3):
                t_x(q, o).wait_send()
        for e in (1, 2, 3):
            t_z(e).wait_send()

    @pl.when(first)
    def _():
        for q in (2, 3):
            t_core(q, n).wait_send()
            for o in (1, 2, 3):
                t_x(q, o, n).wait_send()
        for e in (1, 2, 3):
            @pl.when((z + e) % 4 >= 2)
            def _(e=e):
                t_z(e, n).wait_send()

    for mine, lo in ((others, 0), (first, n)):
        @pl.when(mine)
        def _(lo=lo):
            for s in (0, 1):
                for o in (1, 2, 3):
                    t_fx(s, o, x, lo).wait_send()
                t_fc(s, core, lo).wait_send()
    for o in (1, 2, 3):
        for l in range(4):
            t_gy(l, o, y).wait_send()

        @pl.when((zlo == 0) | ((zlo + o) % 4 != 0))
        def _(o=o):
            t_gz(o, zlo).wait_send()
    for i in CHUNKS:
        for o in (1, 2, 3):
            t_vx(i, o, x).wait_send()
        t_vc(i, core).wait_send()

    @pl.when(zlo == 0)
    def _():
        for o in (1, 2, 3):
            t_gt(o, (zlo + o) % 4).wait_send()
            for i in CHUNKS:
                t_vz(i, o).wait_send()

    @pl.when((row != 0) & (z < 2))
    def _():
        for e in (1, 2, 3):
            t_fz(e).wait_send()

    @pl.when(first)
    def _():
        for o in (1, 2, 3):
            t_gs(o, (y + o) % 4).wait_send()
            for i in CHUNKS:
                t_px(i, o).wait_send()
                t_pz(i, o, z).wait_send()
                t_vy(i, o).wait_send()
            for s in range(4):
                t_rx(s, o).wait_send()
                if s < 2:
                    t_rz(s, o, z).wait_send()

            @pl.when((z + o) % 4 >= 2)
            def _(o=o):
                t_ry(o).wait_send()
        for i in CHUNKS:
            t_pc(i).wait_send()
        for s in range(4):
            t_rc(s).wait_send()


def schur(embedded, diag, hessian):
    spec = pl.BlockSpec(memory_space=pltpu.VMEM)
    dma = pltpu.SemaphoreType.DMA
    pair = lambda *s: [dma(s), dma(s)]
    return pl.pallas_call(
        schur_kernel,
        name="schur",
        out_shape=(
            jax.ShapeDtypeStruct((512, 1024), BF16), jax.ShapeDtypeStruct((512, 1024), BF16),
            jax.ShapeDtypeStruct((512, 512), BF16), jax.ShapeDtypeStruct((512, 512), BF16),
            jax.ShapeDtypeStruct((32, 1024), F32),
        ),
        in_specs=[spec, spec, pl.BlockSpec(memory_space=pltpu.HBM)],
        out_specs=(spec,) * 5,
        scratch_shapes=[
            VM((512, 512), F32), VM((2, 4, 2, 32, 1024), F32), VM((4, 4, 32, 512), F32),
            VM((16, 32, 1024), BF16), dma(()),
            VM((4, 4, 2, 32, 1024), F32), VM((4, 4, 2, 16, 512), F32), VM((4, 4, 2, 32, 512), F32),
            VM((4, 4, 32, 1024), F32), VM((4, 4, 32, 1024), F32),
            VM((3, 4, 32, 1024), F32), VM((4, 32, 1024), F32), VM((3, 32, 1024), F32),
            VM((4, 4, 2, 16, 512), F32),
            VM((4, 4, 16, 512), F32), VM((4, 4, 16, 512), F32), VM((3, 4, 16, 512), F32), VM((4, 4, 16, 512), F32),
            VM((4, 4, 32, 512), F32), VM((4, 4, 32, 512), F32), VM((3, 4, 32, 512), F32), VM((4, 4, 32, 512), F32),
            VM((3, 32, 512), F32), VM((4, 4, 32, 512), F32),
            VM((4, 128, 128), F32), VM((4, 32, 128), F32), VM((128, 512), F32),
            *pair(4), *pair(4, 3), *pair(3),
            dma((3,)), dma((2,)), *pair(2, 3), *pair(2),
            dma((3,)), dma((1,)), dma((3,)), dma((1,)), *pair(3), *pair(4, 3),
            *pair(4), *pair(4, 3), *pair(4, 3), *pair(4), *pair(4, 3), *pair(2, 3), *pair(3),
            dma((4, 3)), dma((4,)), dma((4, 3)), dma((4,)), *pair(4, 3), *pair(4),
        ],
        compiler_params=pltpu.CompilerParams(
            collective_id=0, has_side_effects=True, vmem_limit_bytes=40 * 2**20
        ),
    )(embedded, diag, in_hbm(hessian))


def split(a):
    hi = a.astype(BF16)
    return hi, (a - hi.astype(F32)).astype(BF16)


def dot3(a, b, trans=False):
    dims = (((1,), (1 if trans else 0,)), ((), ()))
    mm = lambda p, q: lax.dot_general(p, q, dims, preferred_element_type=F32)
    (ah, al), (bh, bl) = a, b
    return mm(ah, bh) + (mm(ah, bl) + mm(al, bh))


def apply_kernel(uh, ul, vh, vl, hess_ref, share_ref, out_ref):
    row = lax.axis_index("row")
    col = lax.axis_index("col")
    at = pl.program_id(0)
    rows = pl.ds(pl.multiple_of(at * 128, 128), 128)
    update = dot3((vh[rows, :], vl[rows, :]), (uh[...], ul[...]))
    lane = lax.broadcasted_iota(jnp.int32, (1, 1024), 1)
    for q in range(4):
        band = at * 4 + q
        schur = hess_ref[q].astype(F32) + jnp.where(band == row, share_ref[...], 0.0)
        keep = (band * 1024 + col * 32 >= PW) & (row * 1024 + lane >= PW)
        out_ref[q] = jnp.where(keep, schur - update[32 * q:32 * (q + 1), :], 0.0)


def apply(uh, ul, vh, vl, hessian, share):
    whole = lambda *s: pl.BlockSpec(s, lambda i: (0,) * len(s))
    return pl.pallas_call(
        apply_kernel,
        name="apply",
        grid=(4,),
        out_shape=jax.ShapeDtypeStruct((16, 32, 1024), F32),
        in_specs=[
            whole(512, 1024), whole(512, 1024), whole(512, 512), whole(512, 512),
            pl.BlockSpec((4, 32, 1024), lambda i: (i, 0, 0)), whole(32, 1024),
        ],
        out_specs=pl.BlockSpec((4, 32, 1024), lambda i: (i, 0, 0)),
        compiler_params=pltpu.CompilerParams(
            dimension_semantics=("arbitrary",), vmem_limit_bytes=40 * 2**20
        ),
    )(uh, ul, vh, vl, hessian, share)


def local(coupling, kinv, counts, granules, hessian, reg):
    embedded, diag = embed(coupling[0], kinv[0], counts, granules, reg)
    uh, ul, vh, vl, share = schur(embedded, diag, hessian)
    return apply(uh, ul, vh, vl, hessian, share)


def solution(mesh):
    return jax.shard_map(
        local,
        mesh=mesh,
        in_specs=(
            P(("row", "col"), None, None),
            P(("row", "col"), None, None),
            P(("row", "col")),
            P(("row", "col"), None),
            P(None, "col", "row"),
            P("row"),
        ),
        out_specs=P(None, "col", "row"),
        check_vma=False,
    )
```
